32 devices in a mesh: fsdp: 4 (over y, x), ctx: 2 (over core), tp: 4 (over z).
Axes of the slice: x: 2, y: 2, z: 4, core: 2. Of those that a mesh axis runs over, the one named last changes fastest.
Arguments:
- tokens: bfloat16 [3072, 2048], P(('fsdp', 'ctx')), may hold values from -6 to 6
- segment_ids: int32 [4, 768], P('fsdp'), may hold values from 0 to 5, never falling along the last dimension, each value on 1 to 576 neighbouring positions
- routes: int32 [3072, 8], P(('fsdp', 'ctx')), may hold values from 0 to 31, all different within a row; in each aligned block of 384 rows (0 to 383, 384 to 767, ...) at most 144 rows name the same one
- norm1_gain: bfloat16 [2048], P(('fsdp', 'ctx')), may hold values from 0.5 to 1.5
- q_weight: bfloat16 [2048, 2048], P(('fsdp', 'ctx'), 'tp'), may hold values from -0.125 to 0.125
- k_weight: bfloat16 [2048, 2048], P(('fsdp', 'ctx'), 'tp'), may hold values from -0.125 to 0.125
- v_weight: bfloat16 [2048, 2048], P(('fsdp', 'ctx'), 'tp'), may hold values from -0.125 to 0.125
- q_gain: bfloat16 [128], P(('fsdp', 'ctx')), may hold values from 1 to 2
- k_gain: bfloat16 [128], P(('fsdp', 'ctx')), may hold values from 0.5 to 1.5
- out_weight: bfloat16 [2048, 2048], P(('fsdp', 'ctx'), 'tp'), may hold values from -1.5 to 1.5
- norm2_gain: bfloat16 [2048], P(('fsdp', 'ctx')), may hold values from 0.5 to 1.5
- router_weight: bfloat16 [2048, 32], P(('fsdp', 'ctx')), may hold values from -0.0625 to 0.0625
- gate_weights: bfloat16 [32, 2048, 1024], P(('fsdp', 'ctx'), None, 'tp'), may hold values from -0.125 to 0.125
- up_weights: bfloat16 [32, 2048, 1024], P(('fsdp', 'ctx'), None, 'tp'), may hold values from -0.125 to 0.125
- down_weights: bfloat16 [32, 1024, 2048], P(('fsdp', 'ctx'), 'tp'), may hold values from -0.75 to 0.75
- out_cotangent: bfloat16 [3072, 2048], P(('fsdp', 'ctx')), may hold values from -6 to 6
Outputs:
- output: bfloat16 [3072, 2048], P(('fsdp', 'ctx'))
- input_grad: bfloat16 [3072, 2048], P(('fsdp', 'ctx'))
- norm1_gain_grad: float32 [2048], P(('fsdp', 'ctx'))
- q_weight_grad: float32 [2048, 2048], P(('fsdp', 'ctx'), 'tp')
- k_weight_grad: float32 [2048, 2048], P(('fsdp', 'ctx'), 'tp')
- v_weight_grad: float32 [2048, 2048], P(('fsdp', 'ctx'), 'tp')
- q_gain_grad: float32 [128], P(('fsdp', 'ctx'))
- k_gain_grad: float32 [128], P(('fsdp', 'ctx'))
- out_weight_grad: float32 [2048, 2048], P(('fsdp', 'ctx'), 'tp')
- norm2_gain_grad: float32 [2048], P(('fsdp', 'ctx'))
- router_weight_grad: float32 [2048, 32], P(('fsdp', 'ctx'))
- gate_weights_grad: float32 [32, 2048, 1024], P(('fsdp', 'ctx'), None, 'tp')
- up_weights_grad: float32 [32, 2048, 1024], P(('fsdp', 'ctx'), None, 'tp')
- down_weights_grad: float32 [32, 1024, 2048], P(('fsdp', 'ctx'), 'tp')
The draws below stay inside these ranges and needn't reach their ends.
Inputs may be any that keep to these rules, and one draw needn't show every extreme that they name: In the rows of one device no expert is named by more than 144 routes, a bound that some block reaches. `segment_ids`: along a sequence the numbers never fall; a document has 1 to 576 tokens, and one of each sequence has exactly that many.
All inputs are finite; a program needn't handle non-finite values.
Results may differ from the reference program's by a relative error of at most 0.03.
Values may be sent and summed in bfloat16 or wider, within the bound.
No kernel may reach another device: no remote copies, remote signals or barrier semaphores. Data moves between devices by JAX's collectives and lax.ppermute only.
A program may use at most 384 MiB of HBM per device.

```python
import math
import jax
import jax.numpy as jnp
import numpy as np
from jax import lax

D = 2048
H = 16
HD = 128
FFE = 1024
TOP = 8
DOCS = 6
TOK_DEV = 384
NBLK = 8
EXPERTS = 32
SEQ = 768
SEQS = 4
TOKENS = 3072
CAP = 144
N_TP = 4


def steps_of(key, extent, cuts, low, high):
    level, own = 1.0, jax.random.fold_in(key, 6)
    for axis_at, blocks in cuts:
        heights = jnp.exp(jax.random.uniform(jax.random.fold_in(own, axis_at), (blocks,), jnp.float32, low / len(cuts), high / len(cuts)))
        level = level * jnp.repeat(heights, extent[axis_at] // blocks).reshape([-1 if axis == axis_at else 1 for axis in range(len(extent))])
    return level


def profile(number_of, total, bound, lean):
    weights = [(1 << 20) // math.isqrt(grade ** lean) + 1 for grade in range(2, number_of + 1)]
    surplus, holding = total - bound - (number_of - 1), [1] * (number_of - 1)
    while surplus > 0:
        free = [i for i in range(number_of - 1) if holding[i] < bound]
        whole, left = sum([weights[i] for i in free]), surplus
        for i in free:
            more = min(bound - holding[i], max(1, left * weights[i] // whole), surplus)
            holding[i] = holding[i] + more
            surplus = surplus - more
    return np.array([bound] + holding)


def ragged(stream_key, number_of, total, limit, slope):
    if number_of == 2:
        one = jax.random.randint(stream_key, (), max(1, total - limit), min(limit, total - 1) + 1)
        return jnp.stack([one, total - one])
    tallies = jnp.asarray(profile(number_of, total, limit, slope), jnp.int32)
    twos = (number_of - 1) // 2
    donor, receiver = tallies[1:1 + 2 * twos:2], tallies[2:2 + 2 * twos:2]
    room = jnp.minimum(donor - 1, limit - receiver)
    shifted = jax.random.randint(jax.random.fold_in(stream_key, 1), (twos,), 0, 1 << 20) % (room + 1)
    tallies = tallies.at[1:1 + 2 * twos:2].set(donor - shifted).at[2:2 + 2 * twos:2].set(receiver + shifted)
    return tallies[jax.random.permutation(jax.random.fold_in(stream_key, 2), number_of)]


def deal_out(own_key, own, number, rows, amount, top, most, skew):
    sequence = jax.random.permutation(own_key, amount)
    heavy_load, ordinary = shares(amount, rows * top, most, skew, True), shares(amount, rows * top, most, skew, False)
    places = jnp.arange(amount)

    def named(lengths, offset_by):
        used = int((lengths > 0).sum())
        fixed = max(1, used // 4)
        moved = fixed + (places - fixed + offset_by * (used - fixed)) % max(1, amount - fixed)
        return jnp.zeros((amount,), jnp.int32).at[sequence[jnp.where(places < fixed, places, moved)]].set(jnp.asarray(lengths, jnp.int32))

    lengths = jnp.where(number % 4 == 0, named(heavy_load, number // 4), named(ordinary, number - number // 4 - 1))
    mixed = jax.random.permutation(jax.random.fold_in(own, 3), amount)
    source_of, taker = mixed[0:amount // 2 * 2:2], mixed[1:amount // 2 * 2:2]
    margin = jnp.minimum(lengths[source_of] - 1, most - lengths[taker]) // 2
    margin = jnp.where((source_of == sequence[0]) | (taker == sequence[0]) | (lengths[taker] == 0), 0, jnp.maximum(margin, 0))
    moved = jax.random.randint(jax.random.fold_in(own, 4), (amount // 2,), 0, 1 << 20) % (margin + 1)
    lengths = lengths.at[source_of].add(-moved).at[taker].add(moved)
    members = jnp.searchsorted(jnp.cumsum(lengths), jnp.arange(rows * top), side="right").astype(jnp.int32)
    grid = members.reshape(top, rows).T
    grid = grid[jax.random.permutation(jax.random.fold_in(own, 1), rows)]
    offset_by = jax.random.randint(jax.random.fold_in(own, 2), (rows, 1), 0, top)
    return jnp.take_along_axis(grid, (jnp.arange(top)[None, :] + offset_by) % top, axis=1)


def shares(number_of, total, most, skew, full):
    weights = [(1 << 20) // math.isqrt(rank ** skew) + 1 for rank in range(1, number_of + 1)]
    largest = most if full else min(most, max(-(-total // number_of), total * weights[0] // sum(weights)))
    least = 1 if total - largest >= number_of - 1 else 0
    given, rest = [largest] + [least] * (number_of - 1), total - largest - least * (number_of - 1)
    while rest > 0:
        candidates = [i for i in range(1, number_of) if given[i] < largest] or [i for i in range(1, number_of) if given[i] < most]
        whole, remaining = sum([weights[i] for i in candidates]), rest
        for i in candidates:
            addition = min(most - given[i], max(1, remaining * weights[i] // whole), rest)
            given[i] = given[i] + addition
            rest = rest - addition
    return np.array(given)


def gaussian(rng, shape, scale, limit, cuts=(), kind=jnp.bfloat16):
    values = jax.random.normal(rng, shape, jnp.float32) * scale
    if len(cuts) > 0:
        values = steps_of(rng, shape, cuts, -0.22, 0.18) * values
    return jnp.clip(values, min=-limit, max=limit).astype(kind)


def setup_inputs(seed: int = 0) -> dict:
    key_of = jax.random.split(jax.random.key(seed), 17)
    tokens = gaussian(key_of[0], (TOKENS, D), 1.0, 6.0, ((0, 8),))
    segment_ids = jax.vmap(lambda own: jnp.searchsorted(jnp.cumsum(ragged(own, DOCS, SEQ, 3 * SEQ // 4, 2)), jnp.arange(SEQ), side="right"))(jax.random.split(key_of[1], SEQS)).reshape((SEQS, SEQ)).astype(jnp.int32)
    routes_keys = jax.random.split(jax.random.fold_in(key_of[2], 1), TOKENS // TOK_DEV)
    routes_turns = jax.random.permutation(jax.random.fold_in(key_of[2], 3), TOKENS // TOK_DEV)
    routes = jax.vmap(lambda own, number: deal_out(jax.random.fold_in(key_of[2], 2), own, number, TOK_DEV, EXPERTS, TOP, CAP, 1))(routes_keys, routes_turns).reshape((TOKENS, TOP))
    norm1_gain = jnp.clip(0.5 + 1.0 * jax.random.uniform(key_of[3], (D,), jnp.float32) ** steps_of(key_of[3], (D,), ((0, 8),), -0.2, 0.2), 0.5, 1.5).astype(jnp.bfloat16)
    q_weight = gaussian(key_of[4], (D, H * HD), D ** -0.5, 0.125, ((0, 8), (1, 4)))
    k_weight = gaussian(key_of[5], (D, H * HD), D ** -0.5, 0.125, ((0, 8), (1, 4)))
    v_weight = gaussian(key_of[6], (D, H * HD), D ** -0.5, 0.125, ((0, 8), (1, 4)))
    q_gain = jnp.clip(1.0 + 1.0 * jax.random.uniform(key_of[7], (HD,), jnp.float32) ** steps_of(key_of[7], (HD,), ((0, 8),), -0.2, 0.2), 1.0, 2.0).astype(jnp.bfloat16)
    k_gain = jnp.clip(0.5 + 1.0 * jax.random.uniform(key_of[8], (HD,), jnp.float32) ** steps_of(key_of[8], (HD,), ((0, 8),), -0.2, 0.2), 0.5, 1.5).astype(jnp.bfloat16)
    out_weight = gaussian(key_of[9], (D, H * HD), 16 ** -0.5, 1.5, ((0, 8), (1, 4)))
    norm2_gain = jnp.clip(0.5 + 1.0 * jax.random.uniform(key_of[10], (D,), jnp.float32) ** steps_of(key_of[10], (D,), ((0, 8),), -0.2, 0.2), 0.5, 1.5).astype(jnp.bfloat16)
    router_weight = gaussian(key_of[11], (D, EXPERTS), (4 * D) ** -0.5, 0.0625, ((0, 8),))
    gate_weights = gaussian(key_of[12], (EXPERTS, D, FFE), D ** -0.5, 0.125, ((0, 8), (2, 4)))
    up_weights = gaussian(key_of[13], (EXPERTS, D, FFE), D ** -0.5, 0.125, ((0, 8), (2, 4)))
    down_weights = gaussian(key_of[14], (EXPERTS, FFE, D), (FFE // 16) ** -0.5, 0.75, ((0, 8), (1, 4)))
    out_cotangent = gaussian(key_of[15], (TOKENS, D), 1.0, 6.0, ((0, 8),))
    return dict(tokens=tokens, segment_ids=segment_ids, routes=routes, norm1_gain=norm1_gain, q_weight=q_weight, k_weight=k_weight, v_weight=v_weight, q_gain=q_gain, k_gain=k_gain, out_weight=out_weight, norm2_gain=norm2_gain, router_weight=router_weight, gate_weights=gate_weights, up_weights=up_weights, down_weights=down_weights, out_cotangent=out_cotangent)


eps = 1e-06
rope_base = 10000.0

@jax.custom_vjp
def low(v):
    return lax.optimization_barrier(v.astype(jnp.bfloat16)).astype(jnp.float32)

@jax.custom_vjp
def low_back(v):
    return v

def low_keep(v):
    return (low(v), None)

def low_pass(kept, grad):
    return (grad,)

def back_keep(v):
    return (v, None)

def back_low(kept, grad):
    return (low(grad),)
low.defvjp(low_keep, low_pass)
low_back.defvjp(back_keep, back_low)

def matmul(left, right):
    return jnp.dot(left, right, precision=lax.Precision.HIGHEST, preferred_element_type=jnp.float32)

def rms_scale(values):
    return lax.rsqrt(lax.optimization_barrier(jnp.mean(values * values, axis=-1, keepdims=True)) + eps)

def rotary_tables(positions, width):
    half = width // 2
    freqs = rope_base ** (-(jnp.arange(half, dtype=jnp.float32) * 2.0) / width)
    angles = positions.astype(jnp.float32)[:, None] * freqs[None, :]
    return (jnp.cos(angles), jnp.sin(angles))

def rotate(values, cosine, sine):
    half = values.shape[-1] // 2
    first = values[..., :half]
    second = values[..., half:]
    cosine = cosine[:, None, :]
    sine = sine[:, None, :]
    return jnp.concatenate([first * cosine - second * sine, second * cosine + first * sine], axis=-1)

def route_slots(routes):
    picks = (routes.reshape(-1, TOK_DEV * TOP)[:, :, None] == jnp.arange(EXPERTS, dtype=jnp.int32)[None, None, :]).astype(jnp.int32)
    counts = jnp.cumsum(picks, axis=1)
    return (lax.optimization_barrier(jnp.sum(picks * counts, axis=-1)) - 1).astype(jnp.int32).reshape(routes.shape)

def forward(tokens, norm1_gain, q_weight, k_weight, v_weight, q_gain, k_gain, out_weight, norm2_gain, router_weight, gate_weights, up_weights, down_weights, segment_ids, routes, slots):
    width = H * HD
    normed = low(tokens * rms_scale(tokens) * norm1_gain)
    query_raw = low_back(matmul(normed, q_weight)).reshape(TOKENS, H, HD)
    key_raw = low_back(matmul(normed, k_weight)).reshape(TOKENS, H, HD)
    values = low(low_back(matmul(normed, v_weight))).reshape(SEQS, SEQ, H, HD)
    cosine, sine = rotary_tables(jnp.tile(jnp.arange(SEQ, dtype=jnp.int32), SEQS), HD)
    queries = low(rotate(query_raw * rms_scale(query_raw) * q_gain, cosine, sine) * HD ** (-0.5)).reshape(SEQS, SEQ, H, HD)
    keys = low(rotate(key_raw * rms_scale(key_raw) * k_gain, cosine, sine)).reshape(SEQS, SEQ, H, HD)

    def attend(pieces):
        query, key, value, segment = pieces
        scores = low_back(jnp.einsum('qhd,khd->hqk', query, key, precision=lax.Precision.HIGHEST))
        same = segment[:, None] == segment[None, :]
        scores = jnp.where(same[None], scores, -1e+30)
        peak = lax.optimization_barrier(jnp.max(scores, axis=-1, keepdims=True))
        exponentials = jnp.exp(scores - peak)
        probs = low(exponentials / lax.optimization_barrier(jnp.sum(exponentials, axis=-1, keepdims=True)))
        return jnp.einsum('hqk,khd->qhd', probs, value, precision=lax.Precision.HIGHEST).reshape(SEQ, width)
    mixed = lax.map(jax.checkpoint(attend), (queries, keys, values, segment_ids))
    attended = low(low_back(mixed.reshape(TOKENS, width)))
    residual = tokens + low_back(matmul(attended, out_weight.T))
    hidden_in = low(residual * rms_scale(residual) * norm2_gain)
    logits = low_back(matmul(hidden_in, router_weight))
    chosen = jnp.take_along_axis(logits, routes, axis=1)
    gates = jax.nn.softmax(chosen, axis=-1)
    slice_width = FFE // N_TP
    gate_split = gate_weights.reshape(EXPERTS, D, N_TP, slice_width).transpose(2, 0, 1, 3)
    up_split = up_weights.reshape(EXPERTS, D, N_TP, slice_width).transpose(2, 0, 1, 3)
    down_split = down_weights.reshape(EXPERTS, N_TP, slice_width, D).transpose(1, 0, 2, 3)

    def block(pieces):
        rows_in, block_routes, block_slots, block_gates = pieces
        sent = jnp.zeros((EXPERTS, CAP, D), jnp.float32).at[block_routes.reshape(-1), block_slots.reshape(-1)].set(jnp.repeat(rows_in, TOP, axis=0))
        copies = low_back(jnp.broadcast_to(sent[None], (N_TP, EXPERTS, CAP, D)))
        gate = low_back(jnp.einsum('tecd,tedf->tecf', copies, gate_split, precision=lax.Precision.HIGHEST))
        upper = low_back(jnp.einsum('tecd,tedf->tecf', copies, up_split, precision=lax.Precision.HIGHEST))
        hidden = low(jax.nn.silu(gate) * upper)
        parts = low(low_back(jnp.einsum('tecf,tefd->tecd', hidden, down_split, precision=lax.Precision.HIGHEST)))
        produced = lax.optimization_barrier(jnp.sum(parts, axis=0))
        picked = produced[block_routes, block_slots]
        return lax.optimization_barrier(jnp.sum(block_gates[:, :, None] * picked, axis=1))
    branch = lax.map(jax.checkpoint(block), (hidden_in.reshape(NBLK, TOK_DEV, D), routes.reshape(NBLK, TOK_DEV, TOP), slots.reshape(NBLK, TOK_DEV, TOP), gates.reshape(NBLK, TOK_DEV, TOP)))
    return residual + branch.reshape(TOKENS, D)

def reference(tokens, segment_ids, routes, norm1_gain, q_weight, k_weight, v_weight, q_gain, k_gain, out_weight, norm2_gain, router_weight, gate_weights, up_weights, down_weights, out_cotangent):
    slots = route_slots(routes)
    floats = [array.astype(jnp.float32) for array in (tokens, norm1_gain, q_weight, k_weight, v_weight, q_gain, k_gain, out_weight, norm2_gain, router_weight, gate_weights, up_weights, down_weights)]

    def wrapped(*arrays):
        return forward(*arrays, segment_ids, routes, slots)
    result, pullback = jax.vjp(wrapped, *floats)
    grads = pullback(out_cotangent.astype(jnp.float32))
    return (result.astype(jnp.bfloat16), grads[0].astype(jnp.bfloat16), grads[1], grads[2], grads[3], grads[4], grads[5], grads[6], grads[7], grads[8], grads[9], grads[10], grads[11], grads[12])
```

```python
import jax
import jax.numpy as jnp
from jax import lax
from jax.sharding import PartitionSpec as P

D = 2048
HD = 128
TOP = 8
WAVES = 2

eps = 1e-06
rope_base = 10000.0
BF = jnp.bfloat16
F32 = jnp.float32


def f32(a):
    return a.astype(F32)


def bf(a):
    return a.astype(BF)


def mm(a, b):
    return jnp.dot(a, b, preferred_element_type=F32)


def mm_nt(a, b):
    return lax.dot_general(a, b, (((1,), (1,)), ((), ())), preferred_element_type=F32)


def mm_tn(a, b):
    return lax.dot_general(a, b, (((0,), (0,)), ((), ())), preferred_element_type=F32)


def rms_scale(values):
    return lax.rsqrt(jnp.mean(values * values, axis=-1, keepdims=True) + eps)


def rms_back(grad, values, scale, gain):
    normal = values * scale
    weighted = grad * gain
    inner = jnp.mean(weighted * normal, axis=-1, keepdims=True)
    return (scale * (weighted - normal * inner), grad * normal)


def rotary_tables(positions, width):
    half = width // 2
    freqs = rope_base ** (-(jnp.arange(half, dtype=F32) * 2.0) / width)
    angles = positions.astype(F32)[:, None] * freqs[None, :]
    return (jnp.cos(angles), jnp.sin(angles))


def rotate(values, cosine, sine):
    half = values.shape[-1] // 2
    first = values[..., :half]
    second = values[..., half:]
    cosine = cosine[:, None, :]
    sine = sine[:, None, :]
    return jnp.concatenate(
        [first * cosine - second * sine, second * cosine + first * sine], axis=-1
    )


def rotate_back(values, cosine, sine):
    return rotate(values, cosine, -sine)


def swap_ctx(a):
    return lax.ppermute(a, "ctx", [(0, 1), (1, 0)])


def hop_f(a, mask):
    return lax.ppermute(a, "fsdp", [(i, i ^ mask) for i in range(4)])


def owners_f():
    count = lax.axis_size("fsdp")
    if count == 4:
        own = lax.axis_index("fsdp")
        return [own, own ^ 1, own ^ 2, own ^ 3]
    return list(range(count))


def gather_f(a):
    if lax.axis_size("fsdp") == 4:
        half = a.shape[0] // 2
        by_x = hop_f(a, 1)
        by_y = hop_f(a, 2)
        far = jnp.concatenate([hop_f(by_x[:half], 2), hop_f(by_y[half:], 1)], axis=0)
        return [a, by_x, by_y, far]
    whole = lax.all_gather(a, "fsdp", axis=0)
    return [whole[i] for i in range(whole.shape[0])]


def reduce_f(blocks):
    if lax.axis_size("fsdp") == 4:
        near, by_x, by_y, far = blocks
        half = far.shape[0] // 2
        far = bf(far)
        via_x = hop_f(far[:half], 1)
        via_y = hop_f(far[half:], 2)
        send_y = jnp.concatenate([bf(f32(by_y[:half]) + f32(via_x)), bf(by_y[half:])], axis=0)
        send_x = jnp.concatenate([bf(by_x[:half]), bf(f32(by_x[half:]) + f32(via_y))], axis=0)
        return f32(near) + f32(hop_f(send_x, 1)) + f32(hop_f(send_y, 2))
    stacked = jnp.stack([bf(b) for b in blocks])
    return f32(lax.psum_scatter(stacked, "fsdp", scatter_dimension=0, tiled=False))


def assemble_f(a):
    blocks = gather_f(a)
    size = a.shape[0]
    whole = jnp.zeros((size * len(blocks),) + a.shape[1:], a.dtype)
    for owner, block in zip(owners_f(), blocks):
        whole = lax.dynamic_update_slice_in_dim(whole, block, owner * size, 0)
    return whole


def split_f(a):
    size = a.shape[0] // lax.axis_size("fsdp")
    return [lax.dynamic_slice_in_dim(a, owner * size, size) for owner in owners_f()]


def hop_tp(a, mask):
    count = lax.axis_size("tp")
    return lax.ppermute(a, "tp", [(i, i ^ mask) for i in range(count)])


def gather_tp(a):
    own = lax.axis_index("tp")
    size = a.shape[0]
    count = lax.axis_size("tp")
    whole = jnp.zeros((size * count,) + a.shape[1:], a.dtype)
    whole = lax.dynamic_update_slice_in_dim(whole, a, own * size, 0)
    for mask in range(1, count):
        whole = lax.dynamic_update_slice_in_dim(whole, hop_tp(a, mask), (own ^ mask) * size, 0)
    return whole


def reduce_tp(a):
    own = lax.axis_index("tp")
    count = lax.axis_size("tp")
    size = a.shape[0] // count
    total = f32(lax.dynamic_slice_in_dim(a, own * size, size))
    for mask in range(1, count):
        piece = lax.dynamic_slice_in_dim(a, (own ^ mask) * size, size)
        total = total + f32(hop_tp(bf(piece), mask))
    return total


def own_tp(a):
    size = a.shape[0] // lax.axis_size("tp")
    return lax.dynamic_slice_in_dim(a, lax.axis_index("tp") * size, size)


def in_order(mine, other, axis):
    first = lax.axis_index("ctx") == 0
    return jnp.concatenate(
        [jnp.where(first, mine, other), jnp.where(first, other, mine)], axis=axis
    )


def after(value, *deps):
    return lax.optimization_barrier((value,) + deps)[0]


def gather_rows(a):
    pieces = []
    for block in gather_f(a):
        pieces += [block, swap_ctx(block)]
    return pieces


def reduce_rows(pieces):
    blocks = []
    for i in range(0, len(pieces), 2):
        blocks.append(f32(pieces[i]) + f32(swap_ctx(bf(pieces[i + 1]))))
    return reduce_f(blocks)


def local(
    tokens,
    segment_ids,
    routes,
    norm1_gain,
    q_weight,
    k_weight,
    v_weight,
    q_gain,
    k_gain,
    out_weight,
    norm2_gain,
    router_weight,
    gate_weights,
    up_weights,
    down_weights,
    out_cotangent,
):
    rows = tokens.shape[0]
    experts = router_weight.shape[1]
    n_local = gate_weights.shape[0]
    ffe = gate_weights.shape[2]
    width = q_weight.shape[1] // 2
    heads = width // HD
    depth = q_weight.shape[0]
    core = lax.axis_index("ctx")
    group = lax.axis_index("fsdp") * 2 + core
    wave_rows = rows // WAVES

    def halves(w):
        return (
            lax.dynamic_slice_in_dim(w, core * width, width, 1),
            lax.dynamic_slice_in_dim(w, (1 - core) * width, width, 1),
        )

    small = jnp.concatenate(
        [
            router_weight,
            norm1_gain[:, None],
            norm2_gain[:, None],
            jnp.pad(q_gain, (0, depth - q_gain.shape[0]))[:, None],
            jnp.pad(k_gain, (0, depth - k_gain.shape[0]))[:, None],
            jnp.zeros((depth, 128 - experts - 4), BF),
        ],
        axis=1,
    )
    small_all = assemble_f(in_order(small, swap_ctx(small), 0))
    weight_router = small_all[:, :experts]
    gain_one = f32(small_all[:, experts])
    gain_two = f32(small_all[:, experts + 1])
    per = q_gain.shape[0]
    heads_gain = f32(small_all[:, experts + 2 : experts + 4].reshape(-1, depth, 2)[:, :per])
    gain_q = heads_gain[:, :, 0].reshape(-1)
    gain_k = heads_gain[:, :, 1].reshape(-1)

    mine, theirs = zip(*[halves(w) for w in (q_weight, k_weight, v_weight)])
    qkv_mine = jnp.concatenate(mine, axis=1)
    qkv_theirs = jnp.concatenate(theirs, axis=1)
    weight_qkv = assemble_f(in_order(qkv_mine, swap_ctx(qkv_theirs), 0))
    out_mine, out_theirs = halves(out_weight)
    out_block = in_order(out_mine, swap_ctx(out_theirs), 0)
    out_block = after(out_block, weight_qkv)
    weight_out = assemble_f(out_block)
    cotangent = after(out_cotangent, weight_out)
    cot_pieces = [
        gather_rows(cotangent[w * wave_rows : (w + 1) * wave_rows]) for w in range(WAVES)
    ]

    own_start = core * rows
    other_start = (1 - core) * rows
    both = jnp.concatenate([tokens, swap_ctx(tokens)], axis=0)
    inputs = f32(both)
    scale_one = rms_scale(inputs)
    normed = bf(inputs * scale_one * gain_one)
    raw = mm(normed, weight_qkv)
    length = 2 * rows
    query_raw = raw[:, :width].reshape(length, heads, HD)
    key_raw = raw[:, width : 2 * width].reshape(length, heads, HD)
    values = bf(raw[:, 2 * width :]).reshape(length, heads, HD)
    span = jnp.arange(rows, dtype=jnp.int32)
    cosine, sine = rotary_tables(jnp.concatenate([own_start + span, other_start + span]), HD)
    query_scale = rms_scale(query_raw)
    key_scale = rms_scale(key_raw)
    queries = bf(rotate(query_raw * query_scale * gain_q, cosine, sine) * HD ** (-0.5))
    keys = bf(rotate(key_raw * key_scale * gain_k, cosine, sine))
    segments = jnp.concatenate(
        [
            lax.dynamic_slice_in_dim(segment_ids[0], own_start, rows),
            lax.dynamic_slice_in_dim(segment_ids[0], other_start, rows),
        ]
    )
    same = (segments[:, None] == segments[None, :])[None]
    scores = jnp.einsum("qhd,khd->hqk", queries, keys, preferred_element_type=F32)
    scores = jnp.where(same, scores, -1e30)
    peak = jnp.max(scores, axis=-1, keepdims=True)
    exponentials = jnp.exp(scores - peak)
    total = jnp.sum(exponentials, axis=-1, keepdims=True)
    log_total = peak + jnp.log(total)
    probs = bf(exponentials / total)
    attended = bf(
        jnp.einsum("hqk,khd->qhd", probs, values, preferred_element_type=F32).reshape(
            length, width
        )
    )
    attn_part = mm_nt(attended, weight_out)
    attn_other = swap_ctx(bf(attn_part[rows:]))
    attn_sum = bf(attn_part[:rows] + f32(attn_other))

    gate_up = jnp.concatenate(
        [
            jnp.transpose(gate_weights, (1, 0, 2)).reshape(D, n_local * ffe),
            jnp.transpose(up_weights, (1, 0, 2)).reshape(D, n_local * ffe),
        ],
        axis=1,
    )
    down = down_weights.reshape(n_local * ffe, D)
    mids = n_local * ffe
    spread = jnp.repeat(jnp.eye(n_local, dtype=F32), ffe, axis=1)

    residuals, scales, hiddens, gates_all, hid_rows = [], [], [], [], []
    for w in range(WAVES):
        lo = w * wave_rows
        part = reduce_tp(attn_sum[lo : lo + wave_rows])
        residual = f32(own_tp(tokens[lo : lo + wave_rows])) + part
        scale_two = rms_scale(residual)
        hidden = gather_tp(bf(residual * scale_two * gain_two))
        residuals.append(residual)
        scales.append(scale_two)
        hiddens.append(hidden)
        logits = mm(hidden, weight_router)
        picks = (
            routes[lo : lo + wave_rows, :, None]
            == jnp.arange(experts, dtype=jnp.int32)[None, None, :]
        )
        named = jnp.any(picks, axis=1)
        top = jnp.max(jnp.where(named, logits, -jnp.inf), axis=-1, keepdims=True)
        expo = jnp.where(named, jnp.exp(logits - top), 0.0)
        expo = jnp.where(named, expo, 0.0)
        gates = expo / jnp.sum(expo, axis=-1, keepdims=True)
        gates_all.append(gates)
        hid_rows.append((gather_rows(hidden), gather_rows(gates)))

    feature, cots, saved = [], [], []
    for w in range(WAVES):
        hid_pieces, gate_pieces = hid_rows[w]
        x = jnp.concatenate(hid_pieces, axis=0)
        g = jnp.concatenate(cot_pieces[w], axis=0)
        weights = lax.dynamic_slice_in_dim(
            jnp.concatenate(gate_pieces, axis=0), group * n_local, n_local, 1
        )
        wide = jnp.repeat(weights, ffe, axis=1)
        back = mm_nt(g, down)
        both_up = mm(x, gate_up)
        gate = both_up[:, :mids]
        upper = both_up[:, mids:]
        sigma = jax.nn.sigmoid(gate)
        active = gate * sigma
        mid = active * upper
        cot = jnp.sum((mid * back).reshape(-1, n_local, ffe), axis=-1)
        mid_low = bf(mid * wide)
        act_grad = back * wide
        gate_grad = bf(act_grad * upper * sigma * (1.0 + gate * (1.0 - sigma)))
        upper_grad = bf(act_grad * active)
        grads = jnp.concatenate([gate_grad, upper_grad], axis=1)
        part = bf(mm_nt(grads, gate_up))
        count = 2 * lax.axis_size("fsdp")
        pieces = [part[i * wave_rows : (i + 1) * wave_rows] for i in range(count)]
        cot_wide = jnp.zeros((cot.shape[0], experts), F32)
        cot_wide = lax.dynamic_update_slice_in_dim(cot_wide, cot, group * n_local, 1)
        cot_p = [cot_wide[i * wave_rows : (i + 1) * wave_rows] for i in range(count)]
        feature.append(bf(reduce_rows(pieces)))
        cots.append(bf(reduce_rows(cot_p)))
        saved.append((x, g, mid_low, grads))

    branch_grads, logit_grads, residual_grads, gain_two_sum = [], [], [], 0.0
    for w in range(WAVES):
        lo = w * wave_rows
        feature_grad = reduce_tp(feature[w])
        gate_cot = reduce_tp(cots[w])
        gates = own_tp(gates_all[w])
        logit_grad = bf(gates * (gate_cot - jnp.sum(gates * gate_cot, axis=-1, keepdims=True)))
        hidden_grad = feature_grad + mm_nt(logit_grad, weight_router)
        residual_part, terms = rms_back(hidden_grad, residuals[w], scales[w], gain_two)
        residual_grad = f32(own_tp(out_cotangent[lo : lo + wave_rows])) + residual_part
        gain_two_sum = gain_two_sum + jnp.sum(terms, axis=0)
        residual_grads.append(residual_grad)
        branch_grads.append(gather_tp(bf(residual_grad)))
        logit_grads.append(gather_tp(logit_grad))
    branch_own = jnp.concatenate(branch_grads, axis=0)
    branch_grad = jnp.concatenate([branch_own, swap_ctx(branch_own)], axis=0)

    attended_grad = bf(mm(branch_grad, weight_out)).reshape(length, heads, HD)
    again = jnp.einsum("qhd,khd->hqk", queries, keys, preferred_element_type=F32)
    probs_full = jnp.exp(jnp.where(same, again, -1e30) - log_total)
    probs_low = bf(probs_full)
    prob_grad = jnp.einsum("qhd,khd->hqk", attended_grad, values, preferred_element_type=F32)
    inner = jnp.sum(probs_full * prob_grad, axis=-1, keepdims=True)
    score_grad = bf(probs_full * (prob_grad - inner))
    query_grad = jnp.einsum("hqk,khd->qhd", score_grad, keys, preferred_element_type=F32)
    key_grad = jnp.einsum("hqk,qhd->khd", score_grad, queries, preferred_element_type=F32)
    value_grad = bf(
        jnp.einsum("hqk,qhd->khd", probs_low, attended_grad, preferred_element_type=F32)
    )
    query_pre = rotate_back(query_grad, cosine, sine) * HD ** (-0.5)
    query_raw_grad, gain_q_terms = rms_back(query_pre, query_raw, query_scale, gain_q)
    key_pre = rotate_back(key_grad, cosine, sine)
    key_raw_grad, gain_k_terms = rms_back(key_pre, key_raw, key_scale, gain_k)
    raw_grad = jnp.concatenate(
        [
            bf(query_raw_grad).reshape(length, width),
            bf(key_raw_grad).reshape(length, width),
            value_grad.reshape(length, width),
        ],
        axis=1,
    )
    normed_part = mm_nt(raw_grad, weight_qkv)
    normed_other = swap_ctx(bf(normed_part[rows:]))
    normed_sum = bf(normed_part[:rows] + f32(normed_other))
    input_rows, gain_one_sum = [], 0.0
    for w in range(WAVES):
        lo = w * wave_rows
        normed_grad = reduce_tp(normed_sum[lo : lo + wave_rows])
        x_rows = f32(own_tp(tokens[lo : lo + wave_rows]))
        input_part, terms = rms_back(normed_grad, x_rows, rms_scale(x_rows), gain_one)
        gain_one_sum = gain_one_sum + jnp.sum(terms, axis=0)
        input_rows.append(gather_tp(bf(residual_grads[w] + input_part)))
    input_grad = jnp.concatenate(input_rows, axis=0)

    outputs = []
    for w in range(WAVES):
        x, g, mid_low, grads = saved[w]
        branch = bf(mm(mid_low, down))
        count = 2 * lax.axis_size("fsdp")
        pieces = [branch[i * wave_rows : (i + 1) * wave_rows] for i in range(count)]
        branch_own = reduce_tp(bf(reduce_rows(pieces)))
        outputs.append(gather_tp(bf(residuals[w] + branch_own)))
    output = jnp.concatenate(outputs, axis=0)

    x_all = jnp.concatenate([s[0] for s in saved], axis=0)
    g_all = jnp.concatenate([s[1] for s in saved], axis=0)
    mid_all = jnp.concatenate([s[2] for s in saved], axis=0)
    grads_all = jnp.concatenate([s[3] for s in saved], axis=0)
    gate_grads = jnp.stack(
        [mm_tn(x_all, grads_all[:, e * ffe : (e + 1) * ffe]) for e in range(n_local)]
    )
    up_grads = jnp.stack(
        [mm_tn(x_all, grads_all[:, mids + e * ffe : mids + (e + 1) * ffe]) for e in range(n_local)]
    )
    down_grads = mm_tn(mid_all, g_all).reshape(n_local, ffe, D)

    def own_weight(grad):
        mine = reduce_f([bf(b) for b in split_f(grad)])
        keep = lax.dynamic_slice_in_dim(mine, core * depth, depth)
        give = lax.dynamic_slice_in_dim(mine, (1 - core) * depth, depth)
        return keep, f32(swap_ctx(bf(give)))

    out_keep, out_got = own_weight(mm_tn(branch_grad, attended))
    out_grad = in_order(out_keep, out_got, 1)
    qkv_keep, qkv_got = own_weight(mm_tn(normed, raw_grad))
    qkv_grads = [
        in_order(
            qkv_keep[:, i * width : (i + 1) * width], qkv_got[:, i * width : (i + 1) * width], 1
        )
        for i in range(3)
    ]

    router_grad = mm_tn(jnp.concatenate(hiddens, axis=0), jnp.concatenate(logit_grads, axis=0))
    router_own = f32(
        lax.psum_scatter(bf(router_grad), ("fsdp", "ctx"), scatter_dimension=0, tiled=True)
    )
    packed = jnp.concatenate(
        [
            gain_one_sum,
            gain_two_sum,
            jnp.sum(gain_q_terms, axis=(0, 1)),
            jnp.sum(gain_k_terms, axis=(0, 1)),
        ]
    )
    packed = lax.psum(packed, ("fsdp", "ctx", "tp"))
    gain_one_grad = lax.dynamic_slice_in_dim(packed, group * depth, depth)
    gain_two_grad = lax.dynamic_slice_in_dim(packed, D + group * depth, depth)
    gain_q_grad = lax.dynamic_slice_in_dim(packed, 2 * D + group * per, per)
    gain_k_grad = lax.dynamic_slice_in_dim(packed, 2 * D + HD + group * per, per)
    return (
        output,
        input_grad,
        gain_one_grad,
        qkv_grads[0],
        qkv_grads[1],
        qkv_grads[2],
        gain_q_grad,
        gain_k_grad,
        out_grad,
        gain_two_grad,
        router_own,
        gate_grads,
        up_grads,
        down_grads,
    )


def solution(mesh):
    both = ("fsdp", "ctx")
    in_specs = (
        P(both, None),
        P("fsdp", None),
        P(both, None),
        P(both),
        P(both, "tp"),
        P(both, "tp"),
        P(both, "tp"),
        P(both),
        P(both),
        P(both, "tp"),
        P(both),
        P(both, None),
        P(both, None, "tp"),
        P(both, None, "tp"),
        P(both, "tp", None),
        P(both, None),
    )
    out_specs = (
        P(both, None),
        P(both, None),
        P(both),
        P(both, "tp"),
        P(both, "tp"),
        P(both, "tp"),
        P(both),
        P(both),
        P(both, "tp"),
        P(both),
        P(both, None),
        P(both, None, "tp"),
        P(both, None, "tp"),
        P(both, "tp", None),
    )
    return jax.shard_map(local, mesh=mesh, in_specs=in_specs, out_specs=out_specs, check_vma=False)
```

```python
import functools

import jax
import jax.numpy as jnp
from jax import lax
from jax.experimental import pallas as pl
from jax.experimental.pallas import tpu as pltpu
from jax.sharding import PartitionSpec as P

D = 2048
HD = 128
TOP = 8
WAVES = 2
SIDE = 128
LOW = 64
NEG = -1e30

eps = 1e-06
rope_base = 10000.0
BF = jnp.bfloat16
F32 = jnp.float32


def f32(a):
    return a.astype(F32)


def bf(a):
    return a.astype(BF)


def mm(a, b):
    return jnp.dot(a, b, preferred_element_type=F32)


def mm_nt(a, b):
    return lax.dot_general(a, b, (((1,), (1,)), ((), ())), preferred_element_type=F32)


def mm_tn(a, b):
    return lax.dot_general(a, b, (((0,), (0,)), ((), ())), preferred_element_type=F32)


def rotary_tables(positions, width):
    half = width // 2
    freqs = rope_base ** (-(jnp.arange(half, dtype=F32) * 2.0) / width)
    angles = positions.astype(F32)[:, None] * freqs[None, :]
    cosine, sine = jnp.cos(angles), jnp.sin(angles)
    return (
        jnp.concatenate([cosine, cosine], axis=1),
        jnp.concatenate([-sine, sine], axis=1),
    )


def after(value, *deps):
    return lax.optimization_barrier((value, deps))[0]


def swap_ctx(a):
    return lax.ppermute(a, "ctx", [(0, 1), (1, 0)])


def hop_f(a, masks):
    pairs = [(2 * i + c, 2 * (i ^ masks[c]) + c) for i in range(4) for c in range(2)]
    return lax.ppermute(a, ("fsdp", "ctx"), pairs)


NEAR = (1, 2)
SIDEWAYS = (2, 1)


def gather_f(a, gate=()):
    if lax.axis_size("fsdp") == 4:
        first = hop_f(a, NEAR)
        second = hop_f(a, SIDEWAYS)
        relay = after(first, second, *gate)
        return [a, first, second, hop_f(relay, SIDEWAYS)]
    whole = lax.all_gather(a, "fsdp", axis=0)
    return [whole[i] for i in range(whole.shape[0])]


def gather_near(a):
    return [a, hop_f(a, NEAR), hop_f(a, SIDEWAYS)]


def gather_far(near, *order):
    return hop_f(after(near[1], near[2], *order), SIDEWAYS)


def sum_of(terms):
    out = f32(terms[0])
    for term in terms[1:]:
        out = out + f32(term)
    return out


def reduce_start(far):
    return hop_f(bf(sum_of(far)), SIDEWAYS)


def reduce_end(blocks, relayed):
    own, first, second = blocks[:3]
    got_first = hop_f(bf(sum_of(first + [relayed])), NEAR)
    got_second = hop_f(bf(sum_of(second)), SIDEWAYS)
    return list(own) + [got_first, got_second]


def reduce_f(blocks):
    if lax.axis_size("fsdp") == 4:
        return reduce_end(blocks, reduce_start(blocks[3]))
    stacked = jnp.stack([bf(sum_of(b)) for b in blocks])
    return [lax.psum_scatter(stacked, "fsdp", scatter_dimension=0, tiled=False)]


def alike(blocks):
    if lax.axis_size("fsdp") != 4:
        return list(blocks)
    first = lax.axis_index("ctx") == 0
    return [
        blocks[0],
        jnp.where(first, blocks[1], blocks[2]),
        jnp.where(first, blocks[2], blocks[1]),
        blocks[3],
    ]


def order_f(a, axis):
    if lax.axis_size("fsdp") != 4:
        return a
    own = lax.axis_index("fsdp")
    size = a.shape[axis] // 4
    for bit, places in ((1, (1, 0, 3, 2)), (2, (2, 3, 0, 1))):
        moved = jnp.concatenate(
            [lax.slice_in_dim(a, p * size, (p + 1) * size, axis=axis) for p in places], axis=axis
        )
        a = jnp.where((own & bit) != 0, moved, a)
    return a


def hop_tp(a, mask):
    count = lax.axis_size("tp")
    return lax.ppermute(a, "tp", [(i, i ^ mask) for i in range(count)])


def gather_tp(a):
    return [a] + [hop_tp(a, mask) for mask in range(1, lax.axis_size("tp"))]


def in_order(mine, other, axis):
    first = lax.axis_index("ctx") == 0
    return jnp.concatenate(
        [jnp.where(first, mine, other), jnp.where(first, other, mine)], axis=axis
    )


def attention_parts(q_raw, k_raw, gain_q, gain_k, cosine, sine):
    def turned(raw, gain):
        scale = lax.rsqrt(jnp.mean(raw * raw, axis=-1, keepdims=True) + eps)
        normal = raw * scale
        value = normal * gain
        return scale, normal, value * cosine + pltpu.roll(value, HD // 2, 1) * sine

    q_scale, q_normal, q = turned(q_raw, gain_q)
    k_scale, k_normal, k = turned(k_raw, gain_k)
    return q_scale, q_normal, (q * HD ** (-0.5)).astype(BF), k_scale, k_normal, k.astype(BF)


def attention_forward_kernel(q_ref, k_ref, v_ref, gq, gk, cos, sin, row, col, out, q_s):
    _, _, q, _, _, k = attention_parts(q_ref[...], k_ref[...], gq[...], gk[...], cos[...], sin[...])
    v = v_ref[...].astype(BF)
    q_s[...] = q
    tile = 128

    def step(i, carry):
        rows = pl.ds(pl.multiple_of(i * tile, tile), tile)
        scores = mm_nt(q_s[rows, :], k)
        scores = jnp.where(col[rows, :] == row[...], scores, NEG)
        peak = jnp.max(scores, axis=-1, keepdims=True)
        expo = jnp.exp(scores - peak)
        probs = expo / jnp.sum(expo, axis=-1, keepdims=True)
        out[rows, :] = mm(probs.astype(BF), v).astype(BF)
        return carry

    lax.fori_loop(0, q_s.shape[0] // tile, step, 0)


def attention_forward(raw, gain_q, gain_k, cosine, sine, segments, heads):
    length = raw.shape[0]
    table = pl.BlockSpec((length, HD), lambda h: (0, 0))
    gain = pl.BlockSpec((1, HD), lambda h: (0, 0))

    def column(part):
        return pl.BlockSpec((length, HD), lambda h: (0, part * heads + h))

    return pl.pallas_call(
        attention_forward_kernel,
        grid=(heads,),
        in_specs=[column(0), column(1), column(2), gain, gain, table, table]
        + [
            pl.BlockSpec((1, length), lambda h: (0, 0)),
            pl.BlockSpec((length, 1), lambda h: (0, 0)),
        ],
        out_specs=pl.BlockSpec((length, HD), lambda h: (0, h)),
        out_shape=jax.ShapeDtypeStruct((length, heads * HD), BF),
        scratch_shapes=[pltpu.VMEM((length, HD), BF)],
        compiler_params=pltpu.CompilerParams(vmem_limit_bytes=24 << 20),
        cost_estimate=pl.CostEstimate(
            flops=4 * heads * length * length * HD,
            bytes_accessed=heads * length * HD * 14,
            transcendentals=heads * length * length,
        ),
        name="attention_forward",
    )(raw, raw, raw, gain_q, gain_k, cosine, sine, *segments)


def attention_backward_kernel(
    heads, q_ref, k_ref, v_ref, da_ref, gq, gk, cos, sin, row, col, out, gains, q_s, dq_s, dk_s, dv_s
):
    head = pl.program_id(0)
    q_scale, q_normal, q, k_scale, k_normal, k = attention_parts(
        q_ref[...], k_ref[...], gq[...], gk[...], cos[...], sin[...]
    )
    v = v_ref[...].astype(BF)
    q_s[...] = q
    dk_s[...] = jnp.zeros_like(dk_s)
    dv_s[...] = jnp.zeros_like(dv_s)
    tile = 128

    def step(i, carry):
        rows = pl.ds(pl.multiple_of(i * tile, tile), tile)
        qt = q_s[rows, :]
        da = da_ref[rows, :]
        scores = mm_nt(qt, k)
        scores = jnp.where(col[rows, :] == row[...], scores, NEG)
        peak = jnp.max(scores, axis=-1, keepdims=True)
        expo = jnp.exp(scores - peak)
        probs = expo / jnp.sum(expo, axis=-1, keepdims=True)
        prob_grad = mm_nt(da, v)
        inner = jnp.sum(probs * prob_grad, axis=-1, keepdims=True)
        score_grad = (probs * (prob_grad - inner)).astype(BF)
        dq_s[rows, :] = mm(score_grad, k)
        dk_s[...] += mm_tn(score_grad, qt)
        dv_s[...] += mm_tn(probs.astype(BF), da)
        return carry

    lax.fori_loop(0, q_s.shape[0] // tile, step, 0)
    cosine, sine = cos[...], sin[...]

    def back(grad, normal, scale, gain):
        turned = grad * cosine - pltpu.roll(grad, HD // 2, 1) * sine
        weighted = turned * gain
        inner = jnp.mean(weighted * normal, axis=-1, keepdims=True)
        return (scale * (weighted - normal * inner)).astype(BF), jnp.sum(
            turned * normal, axis=0, keepdims=True
        )

    dq, sum_q = back(dq_s[...] * HD ** (-0.5), q_normal, q_scale, gq[...])
    dk, sum_k = back(dk_s[...], k_normal, k_scale, gk[...])

    def place(part, value):
        out[:, pl.ds(pl.multiple_of((part * heads + head) * HD, HD), HD)] = value

    place(0, dq)
    place(1, dk)
    place(2, dv_s[...].astype(BF))

    @pl.when(head == 0)
    def _():
        gains[...] = jnp.zeros_like(gains)

    gains[0:1, :] += sum_q
    gains[1:2, :] += sum_k


def attention_backward(raw, grad, gain_q, gain_k, cosine, sine, segments, heads):
    length = raw.shape[0]
    table = pl.BlockSpec((length, HD), lambda h: (0, 0))
    gain = pl.BlockSpec((1, HD), lambda h: (0, 0))

    def column(part):
        return pl.BlockSpec((length, HD), lambda h: (0, part * heads + h))

    return pl.pallas_call(
        functools.partial(attention_backward_kernel, heads),
        grid=(heads,),
        in_specs=[column(0), column(1), column(2), column(0), gain, gain, table, table]
        + [
            pl.BlockSpec((1, length), lambda h: (0, 0)),
            pl.BlockSpec((length, 1), lambda h: (0, 0)),
        ],
        out_specs=[
            pl.BlockSpec((length, 3 * heads * HD), lambda h: (0, 0)),
            pl.BlockSpec((8, HD), lambda h: (0, 0)),
        ],
        out_shape=[
            jax.ShapeDtypeStruct((length, 3 * heads * HD), BF),
            jax.ShapeDtypeStruct((8, HD), F32),
        ],
        scratch_shapes=[pltpu.VMEM((length, HD), BF)] + [pltpu.VMEM((length, HD), F32)] * 3,
        compiler_params=pltpu.CompilerParams(vmem_limit_bytes=28 << 20),
        cost_estimate=pl.CostEstimate(
            flops=10 * heads * length * length * HD,
            bytes_accessed=heads * length * HD * 20,
            transcendentals=heads * length * length,
        ),
        name="attention_backward",
    )(raw, raw, raw, grad, gain_q, gain_k, cosine, sine, *segments)


def experts_kernel(places, n_tp, n_local, base, offsets, *refs):
    count = len(places)
    xp = refs[:count]
    g_hbm, pick, gate_up_hbm, down_hbm, own, oth, mid_out, grad_out = refs[count : count + 8]
    xs, gs, gate_up, down, gate_s, up_s, back_s, sems = refs[count + 8 :]
    rows = xs.shape[0]
    size = rows // count
    mids = down.shape[0]
    ffe = mids // n_local
    copies = []
    for i in range(count):
        at = pl.ds(i * size, size)
        copies.append(pltpu.make_async_copy(xp[i], xs.at[at], sems.at[i]))
        part = size // n_tp
        for m in range(n_tp):
            core, block, first = places[i]
            there = offsets[core, block] + first + (base[1] ^ m) * part
            copies.append(
                pltpu.make_async_copy(
                    g_hbm.at[pl.ds(pl.multiple_of(there, 8), part)],
                    gs.at[pl.ds(i * size + m * part, part)],
                    sems.at[count + i * n_tp + m],
                )
            )
    loads = []
    for e in range(n_local):
        for h in range(2):
            at = pl.ds(h * mids + e * ffe, ffe)
            loads.append(
                pltpu.make_async_copy(
                    gate_up_hbm.at[:, at], gate_up.at[:, at], sems.at[count * (n_tp + 1) + 3 * e + h]
                )
            )
        at = pl.ds(e * ffe, ffe)
        loads.append(
            pltpu.make_async_copy(down_hbm.at[at], down.at[at], sems.at[count * (n_tp + 1) + 3 * e + 2])
        )
    for c in copies + loads:
        c.start()
    for c in copies:
        c.wait()
    lane = lax.broadcasted_iota(jnp.int32, (1, SIDE), 1)
    half = rows // 2
    own[:, D:] = jnp.zeros((half, SIDE), BF)
    oth[:, D:] = jnp.zeros((half, SIDE), BF)
    tile = 64
    for e in range(n_local):
        for c in loads[3 * e : 3 * e + 3]:
            c.wait()
        at_gate = pl.ds(e * ffe, ffe)
        at_up = pl.ds(mids + e * ffe, ffe)
        gate_s[...] = mm(xs[:, :D], gate_up[:, at_gate])
        up_s[...] = mm(xs[:, :D], gate_up[:, at_up])
        back_s[...] = mm_nt(gs[...], down[at_gate, :])
        column = base[0] + e
        chosen = pick[e]
        for t in range(rows // tile):
            at = pl.ds(t * tile, tile)
            wide = mm(xs[at, D:], chosen)
            gate = gate_s[at, :]
            upper = up_s[at, :]
            back = back_s[at, :]
            sigma = 0.5 + 0.5 * jnp.tanh(0.5 * gate)
            active = gate * sigma
            mid = active * upper
            cot = jnp.sum(mid * back, axis=-1, keepdims=True)
            mid_out[at, at_gate] = (mid * wide).astype(BF)
            grad = back * wide
            grad_out[at, at_gate] = (grad * upper * (sigma + active * (1.0 - sigma))).astype(BF)
            grad_out[at, at_up] = (grad * active).astype(BF)
            high = cot.astype(BF).astype(F32)
            side = jnp.where(lane == column, high, 0.0)
            side = side + jnp.where(lane == column + LOW, cot - high, 0.0)
            to = own if t * tile < half else oth
            there = pl.ds(t * tile % half, tile)
            to[there, D:] = to[there, D:] + side.astype(BF)
    own[:, :D] = mm_nt(grad_out[pl.ds(0, half), :], gate_up[...]).astype(BF)
    oth[:, :D] = mm_nt(grad_out[pl.ds(half, half), :], gate_up[...]).astype(BF)


def experts(x_pieces, g_all, offsets, places, base, pick, gate_up, down):
    count = len(x_pieces)
    n_tp = lax.axis_size("tp")
    size, width = x_pieces[0].shape
    rows = count * size
    n_local = pick.shape[0]
    mids = down.shape[0]
    ffe = mids // n_local
    anywhere = pl.BlockSpec(memory_space=pl.ANY)

    def whole(*shape):
        return pl.BlockSpec(shape, lambda i, b, o: (0,) * len(shape))

    spec = pltpu.PrefetchScalarGridSpec(
        num_scalar_prefetch=2,
        grid=(1,),
        in_specs=[anywhere] * (count + 1) + [whole(*pick.shape), anywhere, anywhere],
        out_specs=[
            whole(rows // 2, width),
            whole(rows // 2, width),
            whole(rows, mids),
            whole(rows, 2 * mids),
        ],
        scratch_shapes=[
            pltpu.VMEM((rows, width), BF),
            pltpu.VMEM((rows, D), BF),
            pltpu.VMEM(gate_up.shape, BF),
            pltpu.VMEM(down.shape, BF),
            pltpu.VMEM((rows, ffe), F32),
            pltpu.VMEM((rows, ffe), F32),
            pltpu.VMEM((rows, ffe), F32),
            pltpu.SemaphoreType.DMA((count * (n_tp + 1) + 3 * n_local,)),
        ],
    )
    return pl.pallas_call(
        functools.partial(experts_kernel, tuple(places), n_tp, n_local),
        grid_spec=spec,
        out_shape=[
            jax.ShapeDtypeStruct((rows // 2, width), BF),
            jax.ShapeDtypeStruct((rows // 2, width), BF),
            jax.ShapeDtypeStruct((rows, mids), BF),
            jax.ShapeDtypeStruct((rows, 2 * mids), BF),
        ],
        compiler_params=pltpu.CompilerParams(vmem_limit_bytes=60 << 20),
        cost_estimate=pl.CostEstimate(
            flops=rows * mids * D * 10,
            bytes_accessed=6 * mids * D + rows * D * 10,
            transcendentals=rows * mids,
        ),
        name="experts",
    )(base, offsets, *x_pieces, g_all, pick, gate_up, down)

def weights_grad_kernel(places, n_tp, counts, offsets, own, *refs):
    n_x = len(places)
    xp = refs[:n_x]
    g_hbm = refs[n_x]
    n_c = len(counts)
    mids = refs[n_x + 1 : n_x + 1 + n_c]
    gates = refs[n_x + 1 + n_c : n_x + 1 + 2 * n_c]
    ups = refs[n_x + 1 + 2 * n_c : n_x + 1 + 3 * n_c]
    rest = refs[n_x + 1 + 3 * n_c :]
    gate_out, up_out, down_out, token, xs, gs, both, mid_s, sems = rest[-9:]
    token[...] = jnp.zeros_like(token)
    ffe = mid_s.shape[1]
    size = xs.shape[0] // n_x

    @pl.when(pl.program_id(0) == 0)
    def _():
        copies = []
        for i in range(n_x):
            at = pl.ds(i * size, size)
            copies.append(pltpu.make_async_copy(xp[i].at[:, pl.ds(0, D)], xs.at[at], sems.at[i]))
            part = size // n_tp
            for m in range(n_tp):
                core, block, first = places[i]
                there = offsets[core, block] + first + (own[0] ^ m) * part
                copies.append(
                    pltpu.make_async_copy(
                        g_hbm.at[pl.ds(pl.multiple_of(there, 8), part)],
                        gs.at[pl.ds(i * size + m * part, part)],
                        sems.at[n_x + i * n_tp + m],
                    )
                )
        for c in copies:
            c.start()
        for c in copies:
            c.wait()

    row = 0
    for c in range(n_c):
        at = pl.ds(row, counts[c])
        both[at, :ffe] = gates[c][...]
        both[at, ffe:] = ups[c][...]
        mid_s[at, :] = mids[c][...]
        row += counts[c]
    wide = 512

    def step(j, carry):
        at = pl.ds(pl.multiple_of(j * wide, wide), wide)
        part = mm_tn(xs[:, at], both[...])
        gate_out[0, at, :] = part[:, :ffe]
        up_out[0, at, :] = part[:, ffe:]
        down_out[0, :, at] = mm_tn(mid_s[...], gs[:, at])
        return carry

    lax.fori_loop(0, D // wide, step, 0)


def weights_grad(
    x_pieces, g_all, offsets, places, mids, grads, first, number, n_local, before
):
    size = x_pieces[0].shape[0]
    rows = size * len(x_pieces)
    ffe = mids[0].shape[1] // n_local
    counts = [m.shape[0] for m in mids]
    anywhere = pl.BlockSpec(memory_space=pl.ANY)

    def columns(count, shift):
        return pl.BlockSpec((count, ffe), lambda e, o, t: (0, shift + first + e))

    tall = pl.BlockSpec((1, D, ffe), lambda e, o, t: (first + e, 0, 0))
    flat = pl.BlockSpec((1, ffe, D), lambda e, o, t: (first + e, 0, 0))
    n_in = 3 + len(x_pieces) + 3 * len(mids)
    n_tp = lax.axis_size("tp")
    return pl.pallas_call(
        functools.partial(weights_grad_kernel, tuple(places), n_tp, tuple(counts)),
        grid_spec=pltpu.PrefetchScalarGridSpec(
            num_scalar_prefetch=2,
            grid=(number,),
            in_specs=[anywhere] * (len(x_pieces) + 1)
            + [columns(c, 0) for c in counts]
            + [columns(c, 0) for c in counts]
            + [columns(c, n_local) for c in counts]
            + [anywhere] * len(before),
            out_specs=[tall, tall, flat, pl.BlockSpec((8, 128), lambda e, o, t: (0, 0))],
            scratch_shapes=[
                pltpu.VMEM((rows, D), BF),
                pltpu.VMEM((rows, D), BF),
                pltpu.VMEM((rows, 2 * ffe), BF),
                pltpu.VMEM((rows, ffe), BF),
                pltpu.SemaphoreType.DMA((len(x_pieces) * (n_tp + 1),)),
            ],
        ),
        out_shape=[
            jax.ShapeDtypeStruct((n_local, D, ffe), F32),
            jax.ShapeDtypeStruct((n_local, D, ffe), F32),
            jax.ShapeDtypeStruct((n_local, ffe, D), F32),
            jax.ShapeDtypeStruct((8, 128), F32),
        ],
        input_output_aliases={n_in + i: i for i in range(len(before))},
        compiler_params=pltpu.CompilerParams(vmem_limit_bytes=62 << 20),
        cost_estimate=pl.CostEstimate(
            flops=6 * rows * D * ffe * number,
            bytes_accessed=4 * rows * D + 12 * D * ffe * number,
            transcendentals=0,
        ),
        name="weights_grad",
    )(offsets, tp_index(), *x_pieces, g_all, *mids, *grads, *grads, *before)


def prepare_kernel(core, q, k, v, o, gain, mine, theirs, out_mine, out_theirs):
    width = out_mine.shape[1]
    scale = gain[...].astype(F32)
    for to, out_to, which in ((mine, out_mine, core[0]), (theirs, out_theirs, 1 - core[0])):
        at = pl.ds(pl.multiple_of(which * width, width), width)
        for i, w in enumerate((q, k, v)):
            to[:, i * width : (i + 1) * width] = (w[:, at].astype(F32) * scale).astype(BF)
        out_to[...] = o[:, at]


def prepare(core, q, k, v, o, gain):
    depth, both = q.shape
    width = both // 2

    def whole(*shape):
        return pl.BlockSpec(shape, lambda i, c: (0,) * len(shape))

    return pl.pallas_call(
        prepare_kernel,
        grid_spec=pltpu.PrefetchScalarGridSpec(
            num_scalar_prefetch=1,
            grid=(1,),
            in_specs=[whole(depth, both)] * 4 + [whole(depth, 1)],
            out_specs=[whole(depth, 3 * width)] * 2 + [whole(depth, width)] * 2,
        ),
        out_shape=[jax.ShapeDtypeStruct((depth, 3 * width), BF)] * 2
        + [jax.ShapeDtypeStruct((depth, width), BF)] * 2,
        compiler_params=pltpu.CompilerParams(vmem_limit_bytes=16 << 20),
        name="prepare",
    )(core[None].astype(jnp.int32), q, k, v, o, gain)


def whole_spec(*shape):
    return pl.BlockSpec(shape, lambda *i: (0,) * len(shape))


ANYWHERE = pl.BlockSpec(memory_space=pl.ANY)


def first_norm_kernel(x, out):
    value = x[...].astype(F32)
    out[...] = (value * lax.rsqrt(jnp.mean(value * value, axis=-1, keepdims=True) + eps)).astype(BF)


def first_norm(x):
    rows = x.shape[0]
    tile = 96
    block = pl.BlockSpec((tile, D), lambda i: (i, 0))
    return pl.pallas_call(
        first_norm_kernel,
        grid=(rows // tile,),
        in_specs=[block],
        out_specs=block,
        out_shape=jax.ShapeDtypeStruct(x.shape, BF),
        compiler_params=pltpu.CompilerParams(vmem_limit_bytes=16 << 20),
        name="first_norm",
    )(x)


def fixed(*shape):
    return pl.BlockSpec(shape, lambda i, own: (0,) * len(shape))


def tp_index():
    return lax.axis_index("tp").astype(jnp.int32)[None]


def place_kernel(count, firsts, size, own, *refs):
    out = refs[-1]
    waves = len(firsts)
    for m in range(count):
        for w, first in enumerate(firsts):
            there = pl.multiple_of((w * count + (own[0] ^ m)) * size, 8)
            out[pl.ds(there, size), :] = refs[m * waves + w][first * size : (first + 1) * size, :]


def place(chunks, firsts, size, *deps):
    arrays = [a for c in chunks for a in c]
    width = arrays[0].shape[1]
    rows = size * len(arrays)
    return pl.pallas_call(
        functools.partial(place_kernel, len(chunks), tuple(firsts), size),
        grid_spec=pltpu.PrefetchScalarGridSpec(
            num_scalar_prefetch=1,
            grid=(1,),
            in_specs=[whole_spec(*a.shape) for a in arrays] + [ANYWHERE] * len(deps),
            out_specs=whole_spec(rows, width),
        ),
        out_shape=jax.ShapeDtypeStruct((rows, width), arrays[0].dtype),
        compiler_params=pltpu.CompilerParams(vmem_limit_bytes=24 << 20),
        name="place",
    )(tp_index(), *arrays, *deps)


def combine_kernel(counts, size, own, *refs):
    at = 0
    outs = refs[sum(sum(c) for c in counts) :]
    for segments, out in zip(counts, outs):
        for i, count in enumerate(segments):
            total = refs[at][...].astype(F32)
            for r in refs[at + 1 : at + count]:
                total = total + r[...].astype(F32)
            out[i * size : (i + 1) * size, :] = total.astype(out.dtype)
            at += count


def combine(outs, size, dtypes=None):
    dtypes = dtypes or [BF] * len(outs)
    terms = [t for segments in outs for s in segments for t in s]
    width = terms[0][0].shape[1]

    def rows(term):
        assert term[1] % size == 0
        at = term[1] // size
        if len(term) == 2:
            return pl.BlockSpec((size, width), lambda i, own: (at, 0))
        return pl.BlockSpec((size, width), lambda i, own: (at + (own[0] ^ term[2]), 0))

    return pl.pallas_call(
        functools.partial(combine_kernel, [[len(s) for s in o] for o in outs], size),
        grid_spec=pltpu.PrefetchScalarGridSpec(
            num_scalar_prefetch=1,
            grid=(1,),
            in_specs=[rows(t) for t in terms],
            out_specs=[fixed(size * len(o), width) for o in outs],
        ),
        out_shape=[
            jax.ShapeDtypeStruct((size * len(o), width), t) for o, t in zip(outs, dtypes)
        ],
        compiler_params=pltpu.CompilerParams(vmem_limit_bytes=20 << 20),
        name="combine",
    )(tp_index(), *[t[0] for t in terms])


def branch_kernel(count, *refs):
    down, out = refs[count:]
    row = 0
    for r in refs[:count]:
        size = r.shape[0]
        out[row : row + size, :] = mm(r[...], down[...]).astype(BF)
        row += size


def branch_rows(parts, half, down):
    sizes = [p.shape[0] // 2 for p in parts]
    mids = down.shape[0]

    def rows(size):
        return pl.BlockSpec((size, mids), lambda i: (half, 0))

    return pl.pallas_call(
        functools.partial(branch_kernel, len(parts)),
        grid=(1,),
        in_specs=[rows(s) for s in sizes] + [whole_spec(mids, D)],
        out_specs=whole_spec(sum(sizes), D),
        out_shape=jax.ShapeDtypeStruct((sum(sizes), D), BF),
        compiler_params=pltpu.CompilerParams(vmem_limit_bytes=28 << 20),
        cost_estimate=pl.CostEstimate(
            flops=2 * sum(sizes) * mids * D,
            bytes_accessed=2 * (sum(sizes) * (mids + D) + mids * D),
            transcendentals=0,
        ),
        name="branch_rows",
    )(*parts, down)


def inward_kernel(n_a, n_b, owners, *refs):
    pieces = refs[:n_a]
    blocks = refs[n_a : n_a + n_b]
    out = refs[-1]
    size = D // n_b
    row = 0
    for a in pieces:
        total = None
        for b in range(n_b):
            at = pl.ds(pl.multiple_of(owners[b] * size, size), size)
            part = mm(a[:, at], blocks[b][:size, :])
            total = part if total is None else total + part
        out[row : row + a.shape[0], :] = total.astype(out.dtype)
        row += a.shape[0]


def inward(pieces, blocks, owners, dtype):
    rows = sum(a.shape[0] for a in pieces)
    width = blocks[0].shape[1]
    return pl.pallas_call(
        functools.partial(inward_kernel, len(pieces), len(blocks)),
        grid_spec=pltpu.PrefetchScalarGridSpec(
            num_scalar_prefetch=1,
            grid=(1,),
            in_specs=[whole_spec(*a.shape) for a in pieces]
            + [whole_spec(*b.shape) for b in blocks],
            out_specs=whole_spec(rows, width),
        ),
        out_shape=jax.ShapeDtypeStruct((rows, width), dtype),
        compiler_params=pltpu.CompilerParams(vmem_limit_bytes=24 << 20),
        cost_estimate=pl.CostEstimate(
            flops=2 * rows * D * width,
            bytes_accessed=2 * (rows * D + D * width) + 4 * rows * width,
            transcendentals=0,
        ),
        name="inward",
    )(owners, *pieces, *blocks)


def outward_kernel(n_b, owners, a, *refs):
    blocks = refs[:n_b]
    out = refs[-1]
    size = D // n_b
    for b in range(n_b):
        at = pl.ds(pl.multiple_of(owners[b] * size, size), size)
        out[:, at] = mm_nt(a[...], blocks[b][:size, :]).astype(out.dtype)


def outward(a, half, blocks, owners, dtype):
    rows, width = a.shape[0] // 2, a.shape[1]
    return pl.pallas_call(
        functools.partial(outward_kernel, len(blocks)),
        grid_spec=pltpu.PrefetchScalarGridSpec(
            num_scalar_prefetch=1,
            grid=(1,),
            in_specs=[pl.BlockSpec((rows, width), lambda i, o: (half, 0))]
            + [whole_spec(*b.shape) for b in blocks],
            out_specs=whole_spec(rows, D),
        ),
        out_shape=jax.ShapeDtypeStruct((rows, D), dtype),
        compiler_params=pltpu.CompilerParams(vmem_limit_bytes=24 << 20),
        cost_estimate=pl.CostEstimate(
            flops=2 * rows * D * width,
            bytes_accessed=2 * (rows * width + D * width) + 4 * rows * D,
            transcendentals=0,
        ),
        name="outward",
    )(owners, a, *blocks)


def matrix_grad_kernel(n_a, n_b, *refs):
    pieces = refs[:n_a]
    grad, out = refs[n_a], refs[-1]
    size = D // n_b
    for b in range(n_b):
        at = slice(b * size, (b + 1) * size)
        total = None
        row = 0
        for a in pieces:
            part = mm_tn(a[:, at], grad[row : row + a.shape[0], :])
            total = part if total is None else total + part
            row += a.shape[0]
        out[at, :] = total.astype(BF)


def matrix_grad(pieces, grad, *deps):
    rows, width = grad.shape
    return pl.pallas_call(
        functools.partial(matrix_grad_kernel, len(pieces), 4),
        grid=(1,),
        in_specs=[whole_spec(*a.shape) for a in pieces]
        + [whole_spec(rows, width)]
        + [ANYWHERE] * len(deps),
        out_specs=whole_spec(D, width),
        out_shape=jax.ShapeDtypeStruct((D, width), BF),
        compiler_params=pltpu.CompilerParams(vmem_limit_bytes=24 << 20),
        cost_estimate=pl.CostEstimate(
            flops=2 * rows * D * width,
            bytes_accessed=2 * (rows * D + D * width + rows * width),
            transcendentals=0,
        ),
        name="matrix_grad",
    )(*pieces, grad, *deps)


def second_norm_kernel(n_got, index, *refs):
    own = refs[0]
    got = refs[1 : 1 + n_got]
    x, gain, router, routes, residual_out, payload_out, gates_out = refs[1 + n_got :]
    residual = own[...]
    for r in got:
        residual = residual + r[...].astype(F32)
    residual = residual + x[...].astype(F32)
    scale = lax.rsqrt(jnp.mean(residual * residual, axis=-1, keepdims=True) + eps)
    hidden = (residual * scale * gain[...]).astype(BF)
    logits = mm_nt(hidden, router[...])
    rows = hidden.shape[0]
    lane = lax.broadcasted_iota(jnp.int32, (rows, SIDE), 1)
    named = lane == routes[:, 0:1]
    for k in range(1, TOP):
        named = named | (lane == routes[:, k : k + 1])
    logits = jnp.where(named, logits, NEG)
    top = jnp.max(logits, axis=-1, keepdims=True)
    expo = jnp.where(named, jnp.exp(logits - top), 0.0)
    gates = expo / jnp.sum(expo, axis=-1, keepdims=True)
    high = gates.astype(BF)
    low = gates - high.astype(F32)
    residual_out[...] = residual
    gates_out[...] = gates
    payload_out[:, :D] = hidden
    payload_out[:, D:] = (high.astype(F32) + pltpu.roll(low, LOW, 1)).astype(BF)


def second_norm(own, got, x, gain, router, routes):
    rows = own.shape[0]
    count = len(got) + 1
    return pl.pallas_call(
        functools.partial(second_norm_kernel, len(got)),
        grid_spec=pltpu.PrefetchScalarGridSpec(
            num_scalar_prefetch=1,
            grid=(1,),
            in_specs=[fixed(rows, D)] * count
            + [fixed(rows, D), fixed(1, D), fixed(SIDE, D), fixed(rows, TOP)],
            out_specs=[fixed(rows, D), fixed(rows, D + SIDE), fixed(rows, SIDE)],
        ),
        out_shape=[
            jax.ShapeDtypeStruct((rows, D), F32),
            jax.ShapeDtypeStruct((rows, D + SIDE), BF),
            jax.ShapeDtypeStruct((rows, SIDE), F32),
        ],
        compiler_params=pltpu.CompilerParams(vmem_limit_bytes=16 << 20),
        name="second_norm",
    )(tp_index(), own, *got, x, gain, router, routes)


def second_norm_back_kernel(n_got, index, *refs):
    own = refs[0]
    got = refs[1 : 1 + n_got]
    residual_in, payload, gates_in, cot, gain, router, grad_out, low_out, small_out = refs[1 + n_got :]
    total = own[...]
    for r in got:
        total = total + r[...].astype(F32)
    side = total[:, D:]
    lane = lax.broadcasted_iota(jnp.int32, side.shape, 1)
    gates = gates_in[...]
    gate_cot = jnp.where(lane < LOW, side + pltpu.roll(side, LOW, 1), 0.0)
    inner = jnp.sum(gates * gate_cot, axis=-1, keepdims=True)
    logit_grad = (gates * (gate_cot - inner)).astype(BF)
    hidden_grad = total[:, :D] + mm(logit_grad, router[...])
    residual = residual_in[...]
    scale = lax.rsqrt(jnp.mean(residual * residual, axis=-1, keepdims=True) + eps)
    normal = residual * scale
    weighted = hidden_grad * gain[...]
    inner = jnp.mean(weighted * normal, axis=-1, keepdims=True)
    grad = cot[...].astype(F32) + scale * (weighted - normal * inner)
    grad_out[...] = grad
    low_out[...] = grad.astype(BF)
    small_out[0:SIDE, :] = mm_tn(logit_grad, payload[:, :D])
    small_out[SIDE : SIDE + 8, :] = jnp.broadcast_to(
        jnp.sum(hidden_grad * normal, axis=0, keepdims=True), (8, D)
    )


def second_norm_back(own, got, residual, payload, gates, cot, gain, router):
    rows = own.shape[0]
    count = len(got) + 1
    return pl.pallas_call(
        functools.partial(second_norm_back_kernel, len(got)),
        grid_spec=pltpu.PrefetchScalarGridSpec(
            num_scalar_prefetch=1,
            grid=(1,),
            in_specs=[fixed(rows, D + SIDE)] * count
            + [fixed(rows, D), fixed(rows, D + SIDE), fixed(rows, SIDE)]
            + [fixed(rows, D), fixed(1, D), fixed(SIDE, D)],
            out_specs=[fixed(rows, D), fixed(rows, D), fixed(SIDE + 8, D)],
        ),
        out_shape=[
            jax.ShapeDtypeStruct((rows, D), F32),
            jax.ShapeDtypeStruct((rows, D), BF),
            jax.ShapeDtypeStruct((SIDE + 8, D), F32),
        ],
        compiler_params=pltpu.CompilerParams(vmem_limit_bytes=20 << 20),
        name="second_norm_back",
    )(tp_index(), own, *got, residual, payload, gates, cot, gain, router)


def input_grad_kernel(n_got, n_waves, index, *refs):
    own = refs[0]
    got = refs[1 : 1 + n_got]
    x_in = refs[1 + n_got : 1 + n_got + n_waves]
    grads = refs[1 + n_got + n_waves : 1 + n_got + 2 * n_waves]
    residual, out = refs[1 + n_got + 2 * n_waves], refs[-1]
    total = own[...]
    for r in got:
        total = total + r[...].astype(F32)
    row = 0
    for x_ref, g in zip(x_in, grads):
        size = g.shape[0]
        weighted = total[row : row + size]
        x = x_ref[...].astype(F32)
        scale = lax.rsqrt(jnp.mean(x * x, axis=-1, keepdims=True) + eps)
        normal = x * scale
        inner = jnp.mean(weighted * normal, axis=-1, keepdims=True)
        out[row : row + size, :] = (g[...] + scale * (weighted - normal * inner)).astype(BF)
        row += size
    out[row:, :] = (residual[...] + total[row:]).astype(BF)


def input_grad_rows(own, got, x, grads, residual, *deps):
    size = residual.shape[0]
    count = len(got) + 1
    waves = len(grads)
    return pl.pallas_call(
        functools.partial(input_grad_kernel, len(got), waves),
        grid_spec=pltpu.PrefetchScalarGridSpec(
            num_scalar_prefetch=1,
            grid=(1,),
            in_specs=[fixed(*own.shape)] * count
            + [fixed(size, D)] * (2 * waves + 1)
            + [ANYWHERE] * len(deps),
            out_specs=fixed(*own.shape),
        ),
        out_shape=jax.ShapeDtypeStruct(own.shape, BF),
        compiler_params=pltpu.CompilerParams(vmem_limit_bytes=20 << 20),
        name="input_grad_rows",
    )(tp_index(), own, *got, *x, *grads, residual, *deps)


def local(
    tokens,
    segment_ids,
    routes,
    norm1_gain,
    q_weight,
    k_weight,
    v_weight,
    q_gain,
    k_gain,
    out_weight,
    norm2_gain,
    router_weight,
    gate_weights,
    up_weights,
    down_weights,
    out_cotangent,
):
    rows = tokens.shape[0]
    n_experts = router_weight.shape[1]
    n_local, _, ffe = gate_weights.shape
    width = q_weight.shape[1] // 2
    heads = width // HD
    depth = q_weight.shape[0]
    per = q_gain.shape[0]
    core = lax.axis_index("ctx")
    place_f = lax.axis_index("fsdp")
    group = place_f * 2 + core
    n_f = lax.axis_size("fsdp")
    n_tp = lax.axis_size("tp")
    wave = rows // WAVES
    chunk = wave // n_tp
    mids = n_local * ffe
    if n_f == 4:
        owners = place_f ^ jnp.stack([0 * core, 1 + core, 2 - core, 0 * core + 3])
    else:
        owners = jnp.arange(n_f)
    owners = owners.astype(jnp.int32)

    if n_f == 4:
        other_owners = place_f ^ jnp.stack([0 * core, 2 - core, 1 + core, 0 * core + 3])
    else:
        other_owners = owners
    cot_rows = rows * jnp.stack([owners * 2 + core, other_owners * 2 + (1 - core)])
    cot_rows = cot_rows.astype(jnp.int32)

    gain_one = f32(norm1_gain)[:, None]
    qkv_mine, qkv_theirs, out_mine, out_theirs = prepare(
        core, q_weight, k_weight, v_weight, out_weight, norm1_gain[:, None]
    )
    small_rows = -(-(n_experts + 16) // 16) * 16
    small = jnp.concatenate(
        [
            jnp.pad(q_gain, (0, depth - per))[None, :],
            jnp.pad(k_gain, (0, depth - per))[None, :],
            norm2_gain[None, :],
            jnp.zeros((13, depth), BF),
            router_weight.T,
            jnp.zeros((small_rows - n_experts - 16, depth), BF),
        ],
        axis=0,
    )
    qkv_block = in_order(qkv_mine, swap_ctx(qkv_theirs), 0)
    tokens, out_cotangent, segment_ids, routes = after(
        (tokens, out_cotangent, segment_ids, routes), qkv_block
    )
    normed_own = first_norm(tokens)
    normed = [normed_own, swap_ctx(normed_own)]
    small_all = lax.all_gather(after(small, normed_own), ("fsdp", "ctx"), axis=0)
    positions = lax.rem(core * rows + jnp.arange(2 * rows, dtype=jnp.int32), 2 * rows)
    cosine, sine = rotary_tables(after(positions, qkv_block), HD)
    segments = lax.dynamic_slice_in_dim(
        jnp.concatenate([segment_ids[0], segment_ids[0]]), core * rows, 2 * rows
    )
    segments = (segments[None, :], segments[:, None])
    base = jnp.stack([group * n_local, lax.axis_index("tp")]).astype(jnp.int32)
    columns = base[0] + jnp.arange(n_local, dtype=jnp.int32)[:, None, None]
    lanes = jnp.arange(SIDE, dtype=jnp.int32)[None, :, None]
    pick = bf(
        jnp.broadcast_to((lanes == columns) | (lanes == columns + LOW), (n_local, SIDE, ffe))
    )
    def rows_of_waves(a):
        own = lax.axis_index("tp") * chunk
        return [lax.dynamic_slice_in_dim(a, w * wave + own, chunk) for w in range(WAVES)]

    x_rows, cot_own, routes_own = [rows_of_waves(a) for a in (tokens, out_cotangent, routes)]
    out_block = in_order(out_mine, swap_ctx(out_theirs), 0)
    qkv_blocks = gather_f(
        qkv_block, (normed_own, cosine, sine, segments, x_rows, cot_own, routes_own, small_all)
    )
    out_blocks = gather_f(after(out_block, qkv_blocks[-1]), (pick, cot_rows))
    cot_all = lax.all_gather(
        after(out_cotangent, qkv_blocks[-1]),
        ("fsdp", "ctx"),
        axis=0,
        tiled=True,
    )
    gain_q = f32(small_all[:, 0, :per].reshape(1, HD))
    gain_k = f32(small_all[:, 1, :per].reshape(1, HD))
    gain_two = f32(small_all[:, 2].reshape(1, D))
    router_wide = jnp.concatenate(
        [
            jnp.swapaxes(small_all[:, 16 : 16 + n_experts], 0, 1).reshape(n_experts, D),
            jnp.zeros((SIDE - n_experts, D), BF),
        ],
        axis=0,
    )
    raw = inward(normed, qkv_blocks, owners, F32)
    attended = attention_forward(raw, gain_q, gain_k, cosine, sine, segments, heads)
    attn_give = outward(attended, 1, out_blocks, owners, BF)
    attn_got = swap_ctx(attn_give)
    attn_keep = outward(after(attended, attn_give), 0, out_blocks, owners, F32)

    def tp_hops(sends):
        return [hop_tp(a, m + 1) for m, a in enumerate(sends)]

    down = down_weights.reshape(mids, D)
    residuals, payloads, gates_own, hid_pieces = [], [], [], []

    def attention_sums(w, *order):
        keep, got = after((attn_keep, attn_got), *order)
        lo = w * wave
        own, *sends = combine(
            [[[(keep, lo, m), (got, lo, m)]] for m in range(n_tp)],
            chunk,
            [F32] + [BF] * (n_tp - 1),
        )
        return own, sends, tp_hops(sends)

    def norm_rows(w, own, got):
        residual, payload, gates = second_norm(
            own, got, x_rows[w], gain_two, router_wide, routes_own[w]
        )
        residuals.append(residual)
        payloads.append(payload)
        gates_own.append(gates)
        return gather_tp(payload)

    def both_cores(a, *order):
        return a, swap_ctx(after(a, *order) if order else a)

    def gather_wave(chunks):
        payload = jnp.concatenate(chunks, axis=0)
        if n_f != 4:
            hid_pieces.append([both_cores(b) for b in gather_f(payload)])
            return payload, None
        near = gather_near(payload)
        hid_pieces.append([both_cores(payload, near[1])])
        return payload, near

    own_rows, sends, got_rows = attention_sums(0)
    gate_in, up_in = after((gate_weights, up_weights), *sends)
    gate_up = jnp.concatenate(
        [
            jnp.transpose(gate_in, (1, 0, 2)).reshape(D, mids),
            jnp.transpose(up_in, (1, 0, 2)).reshape(D, mids),
        ],
        axis=1,
    )
    own_rows = after(own_rows, gate_up, pick)
    payload, near_a = gather_wave(norm_rows(0, own_rows, got_rows))
    own_rows, _, got_rows = attention_sums(1, payload)
    assert WAVES == 2

    kept = []

    def call(w, blocks, *order):
        xs = [hid_pieces[w][b][s] for s in range(2) for b in blocks]
        at = [(s, b, w * wave) for s in range(2) for b in blocks]
        if order:
            xs[0] = after(xs[0], *order)
        own, oth, mid, grads = experts(
            xs, cot_all, cot_rows, at, base, pick, gate_up, down
        )
        kept.append((xs, at, mid, grads, blocks, w))
        return own, oth

    def swapped(blocks, own, oth, *order):
        if order:
            oth = after(oth, *order)
        got = swap_ctx(oth)
        return {b: [(own, i * wave), (got, i * wave)] for i, b in enumerate(blocks)}

    def branch_half(w, s, *order):
        parts = [k[2] for k in kept if k[5] == w]
        places = [b for k in kept if k[5] == w for b in k[4]]
        parts[0] = after(parts[0], *order)
        return branch_rows(parts, s, down), places

    def branch_terms(keep, got, places):
        return {b: [(keep, i * wave), (got, i * wave)] for i, b in enumerate(places)}

    def tied(terms, *order):
        return [(after(terms[0][0], *order), terms[0][1])] + list(terms[1:])

    def shifted(terms, row):
        return [(a, at + row) for a, at in terms]

    def tp_parts(terms, *order):
        terms = tied(terms, *order)
        parts = combine(
            [[shifted(terms, m * chunk)] for m in range(n_tp)], chunk, [F32] + [BF] * (n_tp - 1)
        )
        return parts[0], parts[1:]

    def plain_terms(terms):
        return [a[at : at + wave] for a, at in terms]

    residual_grads, branch_pieces, small_parts = [], [], []

    def norm_back(w, parts, *order):
        own, sends = parts
        residual_grad, low, small_part = second_norm_back(
            after(own, *order) if order else own,
            tp_hops(sends),
            residuals[w],
            payloads[w],
            gates_own[w],
            cot_own[w],
            gain_two,
            router_wide,
        )
        residual_grads.append(residual_grad)
        small_parts.append(small_part)
        return low

    if n_f == 4:
        hid_pieces[0] += [both_cores(a) for a in near_a[1:]]
        far = gather_far(near_a)
        own_a, oth_a = call(0, [0, 1, 2])
        chunks = norm_rows(1, after(own_rows, own_a), got_rows)
        hid_pieces[0].append(both_cores(far, chunks[0]))
        own_f, oth_f = call(0, [3], own_a, chunks[0])
        payload, near_b = gather_wave([after(chunks[0], own_f)] + chunks[1:])
        terms_a = swapped([3], own_f, oth_f, payload)
        terms_a.update(swapped([0, 1, 2], own_a, oth_a, payload))
        give_a, places = branch_half(0, 1, payload)
        branch_got_a = swap_ctx(give_a)
        (far_a,) = combine([[tied(terms_a[3], give_a)]], wave)
        relay_a = hop_f(far_a, SIDEWAYS)
        keep_a, _ = branch_half(0, 0, far_a)
        branch_a = branch_terms(keep_a, branch_got_a, places)

        far = gather_far(near_b, keep_a)
        own_0, oth_0 = call(1, [0], keep_a)
        hid_pieces[1] += [both_cores(a, own_0) for a in near_b[1:]]
        hid_pieces[1].append(both_cores(far, own_0))
        send_1, send_2 = combine(
            [[tied(terms_a[1], own_0) + [(relay_a, 0)]], [terms_a[2]]], wave
        )
        terms_b = swapped([0], own_0, oth_0, send_1)
        feature = terms_a[0] + [(hop_f(send_1, NEAR), 0), (hop_f(send_2, SIDEWAYS), 0)]
        (branch_far,) = combine([[tied(branch_a[3], send_1)]], wave)
        branch_relay = hop_f(branch_far, SIDEWAYS)

        own_1, oth_1 = call(1, [1, 2], send_1, branch_far)
        feature_a = tp_parts(feature, own_1)
        terms_b.update(swapped([1, 2], own_1, oth_1, feature_a[0]))
        send_1, send_2 = combine(
            [[tied(branch_a[1], feature_a[0]) + [(branch_relay, 0)]], [branch_a[2]]], wave
        )
        branch = branch_a[0] + [(hop_f(send_1, NEAR), 0), (hop_f(send_2, SIDEWAYS), 0)]

        own_3, oth_3 = call(1, [3], own_1, send_1)
        low = norm_back(0, feature_a, own_3, branch[-1][0], branch[-2][0])
        terms_b.update(swapped([3], own_3, oth_3, low))
        own_g, *sends = combine(
            [[[(low, 0)], shifted(branch, m * chunk)] for m in range(n_tp)],
            chunk,
            [F32] + [BF] * (n_tp - 1),
        )
        got_g = tp_hops(sends)
        (far_b,) = combine([[tied(terms_b[3], own_g)]], wave)
        relay_b = hop_f(far_b, SIDEWAYS)
        send_1, send_2 = combine(
            [[tied(terms_b[1], far_b) + [(relay_b, 0)]], [terms_b[2]]], wave
        )
        feature = terms_b[0] + [(hop_f(send_1, NEAR), 0), (hop_f(send_2, SIDEWAYS), 0)]
        (out_0,) = combine(
            [[[(residuals[0], 0), (after(own_g, send_1), chunk)] + [(a, chunk) for a in got_g]]],
            chunk,
        )
        branch_own = place([[low]] + [[a] for a in after(tuple(got_g), out_0)], (0,), chunk)
        branch_pieces.append((branch_own, swap_ctx(branch_own)))
        feature_b = tp_parts(tied(feature, out_0))
        give_b, places = branch_half(1, 1, feature_b[0])
        branch_got_b = swap_ctx(give_b)
        keep_b, _ = branch_half(1, 0, give_b)
        branch_b = branch_terms(keep_b, branch_got_b, places)
        (branch_far,) = combine([[branch_b[3]]], wave)
        branch_relay = hop_f(branch_far, SIDEWAYS)
        low = norm_back(1, feature_b)
        send_1, send_2 = combine(
            [[tied(branch_b[1], low) + [(branch_relay, 0)]], [branch_b[2]]], wave
        )
        last_branch = branch_b[0] + [(hop_f(send_1, NEAR), 0), (hop_f(send_2, SIDEWAYS), 0)]
        branch_own = place([[a] for a in gather_tp(low)], (0,), chunk)
        branch_pieces.append((branch_own, swap_ctx(branch_own)))
        out_chunks = gather_tp(after(out_0, branch_own))
        early = (send_1,)
        under = tuple(out_chunks[1:]) + tuple(a for a, _ in last_branch[-2:])
    else:
        for w in range(WAVES):
            if w == 1:
                gather_wave(norm_rows(1, own_rows, got_rows))
            terms = {}
            for b in range(n_f):
                terms.update(swapped([b], *call(w, [b])))
            got = reduce_f([plain_terms(terms[b]) for b in range(n_f)])
            low = norm_back(w, tp_parts([(a, 0) for a in got]))
            branch_own = place([[a] for a in gather_tp(low)], (0,), chunk)
            branch_pieces.append((branch_own, swap_ctx(branch_own)))
            give, places = branch_half(w, 1)
            keep, _ = branch_half(w, 0)
            terms = branch_terms(keep, swap_ctx(give), places)
            got = reduce_f([plain_terms(terms[b]) for b in range(n_f)])
            last_branch = [(a, 0) for a in got]
            if w == 0:
                own, sends = tp_parts(last_branch)
                (out_0,) = combine(
                    [[[(a, 0) for a in (residuals[0], own, *tp_hops(sends))]]], chunk
                )
                out_chunks = gather_tp(out_0)
        early = ()
        under = ()
    branch_grad = [branch_pieces[w][s] for s in range(2) for w in range(WAVES)]
    branch_grad[0] = after(branch_grad[0], *early)

    attended_grad = inward(branch_grad, out_blocks, owners, BF)
    out_grad_part = matrix_grad(branch_grad, attended, attended_grad)
    out_sum = lax.psum_scatter(out_grad_part, "fsdp", scatter_dimension=0, tiled=True)
    raw_grad, gain_terms = attention_backward(
        raw,
        after(attended_grad, out_grad_part),
        gain_q,
        gain_k,
        cosine,
        sine,
        segments,
        heads,
    )
    raw_grad = after(raw_grad, *under)
    normed_give = outward(raw_grad, 1, qkv_blocks, owners, BF)
    normed_got = swap_ctx(normed_give)
    qkv_grad_part = matrix_grad(normed, raw_grad, normed_give)
    qkv_sum = lax.psum_scatter(qkv_grad_part, "fsdp", scatter_dimension=0, tiled=True)
    normed_keep = outward(after(raw_grad, qkv_grad_part), 0, qkv_blocks, owners, F32)

    normed_rows, *normed_sends = combine(
        [
            [
                [(normed_keep, w * wave, m), (normed_got, w * wave, m)]
                for w in range(WAVES)
            ]
            + [shifted(last_branch, m * chunk)]
            for m in range(n_tp)
        ],
        chunk,
        [F32] + [BF] * (n_tp - 1),
    )
    normed_recv = tp_hops(normed_sends)

    small_parts, gain_terms = after((small_parts, gain_terms), *normed_sends)
    def spread(terms):
        return jnp.pad(terms.reshape(2 * n_f, per), ((0, 0), (0, depth - per))).reshape(1, D)

    small_grad = sum(small_parts)
    small_part = jnp.concatenate(
        [
            small_grad[:n_experts],
            small_grad[SIDE : SIDE + 1],
            spread(gain_terms[0]),
            spread(gain_terms[1]),
            jnp.zeros((small_rows - n_experts - 3, D), F32),
        ],
        axis=0,
    )
    small_part = jnp.swapaxes(small_part.reshape(small_rows, 2 * n_f, depth), 0, 1)
    small_sum = lax.psum_scatter(
        small_part.reshape(2 * n_f * small_rows, depth),
        ("fsdp", "ctx"),
        scatter_dimension=0,
        tiled=True,
    )

    def own_weight(mine):
        mine = f32(mine)
        keep = lax.dynamic_slice_in_dim(mine, core * depth, depth)
        give = lax.dynamic_slice_in_dim(mine, (1 - core) * depth, depth)
        return keep, f32(swap_ctx(bf(give)))

    x_pieces = [x for k in kept for x in k[0]]
    places = [p for k in kept for p in k[1]]
    mid_list = [k[2] for k in kept]
    grad_list = [k[3] for k in kept]
    def finish(rows_in, *order):
        rows_out = input_grad_rows(
            normed_rows, rows_in, x_rows, residual_grads, residuals[-1], *order
        )
        return rows_out, gather_tp(rows_out)

    if n_f == 4:
        step = n_local // 2
        x_pieces[0] = after(x_pieces[0], *normed_sends)
        *done, token = weights_grad(
            x_pieces, cot_all, cot_rows, places, mid_list, grad_list, 0, step, n_local, []
        )
        last_rows, last_chunks = finish(normed_recv, token, out_sum, qkv_sum)
        x_pieces[0] = after(x_pieces[0], last_rows)
        qkv_sum, out_sum = after((qkv_sum, out_sum), last_rows)
        *done, token = weights_grad(
            x_pieces, cot_all, cot_rows, places, mid_list, grad_list, step, n_local - step, n_local, done
        )
        ending = (token,)
    else:
        last_rows, last_chunks = finish(normed_recv)
        ending = ()
        x_all = jnp.concatenate([x[:, :D] for x in x_pieces], axis=0)
        own = lax.axis_index("tp")
        g_all = jnp.concatenate(
            [
                lax.dynamic_slice_in_dim(
                    cot_all, cot_rows[s, b] + first + (own ^ m) * chunk, chunk
                )
                for s, b, first in places
                for m in range(n_tp)
            ],
            axis=0,
        )
        grad_all = jnp.concatenate(grad_list, axis=0)
        mid_all = jnp.concatenate(mid_list, axis=0)
        done = [
            jnp.stack(
                [
                    mm_tn(x_all, grad_all[:, s * mids + e * ffe : s * mids + (e + 1) * ffe])
                    for e in range(n_local)
                ]
            )
            for s in range(2)
        ] + [mm_tn(mid_all, g_all).reshape(n_local, ffe, D)]
    input_grad = place([[c] * WAVES for c in last_chunks], range(WAVES), chunk, *ending)
    output = place([[o, c] for o, c in zip(out_chunks, last_chunks)], (0, WAVES), chunk)
    gate_grads, up_grads, down_grads = done

    qkv_keep, qkv_got = own_weight(qkv_sum)
    out_grad = in_order(*own_weight(out_sum), 1)
    plain = [
        in_order(
            qkv_keep[:, i * width : (i + 1) * width], qkv_got[:, i * width : (i + 1) * width], 1
        )
        for i in range(3)
    ]
    qkv_grads = [p * gain_one for p in plain]
    gain_one_part = sum(
        jnp.sum(p * f32(w), axis=1) for p, w in zip(plain, (q_weight, k_weight, v_weight))
    )

    small_sum = jnp.concatenate([small_sum, gain_one_part[None, :]], axis=0)
    small_sum = sum_of(gather_tp(after(small_sum, *last_chunks[1:])))
    return (
        output,
        input_grad,
        small_sum[small_rows],
        qkv_grads[0],
        qkv_grads[1],
        qkv_grads[2],
        small_sum[n_experts + 1, :per],
        small_sum[n_experts + 2, :per],
        out_grad,
        small_sum[n_experts],
        small_sum[:n_experts].T,
        gate_grads,
        up_grads,
        down_grads,
    )


def solution(mesh):
    both = ("fsdp", "ctx")
    in_specs = (
        P(both, None),
        P("fsdp", None),
        P(both, None),
        P(both),
        P(both, "tp"),
        P(both, "tp"),
        P(both, "tp"),
        P(both),
        P(both),
        P(both, "tp"),
        P(both),
        P(both, None),
        P(both, None, "tp"),
        P(both, None, "tp"),
        P(both, "tp", None),
        P(both, None),
    )
    out_specs = (
        P(both, None),
        P(both, None),
        P(both),
        P(both, "tp"),
        P(both, "tp"),
        P(both, "tp"),
        P(both),
        P(both),
        P(both, "tp"),
        P(both),
        P(both, None),
        P(both, None, "tp"),
        P(both, None, "tp"),
        P(both, "tp", None),
    )
    return jax.shard_map(local, mesh=mesh, in_specs=in_specs, out_specs=out_specs, check_vma=False)
```

```python
import functools

import jax
import jax.numpy as jnp
from jax import lax
from jax.experimental import pallas as pl
from jax.experimental.pallas import tpu as pltpu
from jax.sharding import PartitionSpec as P

D = 2048
HD = 128
TOP = 8
WAVES = 2
SIDE = 128
LOW = 64
NEG = -1e30

eps = 1e-06
rope_base = 10000.0
BF = jnp.bfloat16
F32 = jnp.float32


def f32(a):
    return a.astype(F32)


def bf(a):
    return a.astype(BF)


def mm(a, b):
    return jnp.dot(a, b, preferred_element_type=F32)


def mm_nt(a, b):
    return lax.dot_general(a, b, (((1,), (1,)), ((), ())), preferred_element_type=F32)


def mm_tn(a, b):
    return lax.dot_general(a, b, (((0,), (0,)), ((), ())), preferred_element_type=F32)


def rotary_tables(positions, width):
    half = width // 2
    freqs = rope_base ** (-(jnp.arange(half, dtype=F32) * 2.0) / width)
    angles = positions.astype(F32)[:, None] * freqs[None, :]
    cosine, sine = jnp.cos(angles), jnp.sin(angles)
    return (
        jnp.concatenate([cosine, cosine], axis=1),
        jnp.concatenate([-sine, sine], axis=1),
    )


def after(value, *deps):
    return lax.optimization_barrier((value, deps))[0]


def swap_ctx(a):
    return lax.ppermute(a, "ctx", [(0, 1), (1, 0)])


def hop_f(a, masks):
    pairs = [(2 * i + c, 2 * (i ^ masks[c]) + c) for i in range(4) for c in range(2)]
    return lax.ppermute(a, ("fsdp", "ctx"), pairs)


NEAR = (1, 2)
SIDEWAYS = (2, 1)


def gather_f(a, gate=()):
    if lax.axis_size("fsdp") == 4:
        first = hop_f(a, NEAR)
        second = hop_f(a, SIDEWAYS)
        relay = after(first, second, *gate)
        return [a, first, second, hop_f(relay, SIDEWAYS)]
    whole = lax.all_gather(a, "fsdp", axis=0)
    return [whole[i] for i in range(whole.shape[0])]


def gather_near(a):
    return [a, hop_f(a, NEAR), hop_f(a, SIDEWAYS)]


def gather_far(near, *order):
    return hop_f(after(near[1], near[2], *order), SIDEWAYS)


def sum_of(terms):
    out = f32(terms[0])
    for term in terms[1:]:
        out = out + f32(term)
    return out


def reduce_start(far):
    return hop_f(bf(sum_of(far)), SIDEWAYS)


def reduce_end(blocks, relayed):
    own, first, second = blocks[:3]
    got_first = hop_f(bf(sum_of(first + [relayed])), NEAR)
    got_second = hop_f(bf(sum_of(second)), SIDEWAYS)
    return list(own) + [got_first, got_second]


def reduce_f(blocks):
    if lax.axis_size("fsdp") == 4:
        return reduce_end(blocks, reduce_start(blocks[3]))
    stacked = jnp.stack([bf(sum_of(b)) for b in blocks])
    return [lax.psum_scatter(stacked, "fsdp", scatter_dimension=0, tiled=False)]


def alike(blocks):
    if lax.axis_size("fsdp") != 4:
        return list(blocks)
    first = lax.axis_index("ctx") == 0
    return [
        blocks[0],
        jnp.where(first, blocks[1], blocks[2]),
        jnp.where(first, blocks[2], blocks[1]),
        blocks[3],
    ]


def order_f(a, axis):
    if lax.axis_size("fsdp") != 4:
        return a
    own = lax.axis_index("fsdp")
    size = a.shape[axis] // 4
    for bit, places in ((1, (1, 0, 3, 2)), (2, (2, 3, 0, 1))):
        moved = jnp.concatenate(
            [lax.slice_in_dim(a, p * size, (p + 1) * size, axis=axis) for p in places], axis=axis
        )
        a = jnp.where((own & bit) != 0, moved, a)
    return a


def hop_tp(a, mask):
    count = lax.axis_size("tp")
    return lax.ppermute(a, "tp", [(i, i ^ mask) for i in range(count)])


def gather_tp(a):
    return [a] + [hop_tp(a, mask) for mask in range(1, lax.axis_size("tp"))]


def in_order(mine, other, axis):
    first = lax.axis_index("ctx") == 0
    return jnp.concatenate(
        [jnp.where(first, mine, other), jnp.where(first, other, mine)], axis=axis
    )


def attention_parts(q_raw, k_raw, gain_q, gain_k, cosine, sine):
    def turned(raw, gain):
        scale = lax.rsqrt(jnp.mean(raw * raw, axis=-1, keepdims=True) + eps)
        normal = raw * scale
        value = normal * gain
        return scale, normal, value * cosine + pltpu.roll(value, HD // 2, 1) * sine

    q_scale, q_normal, q = turned(q_raw, gain_q)
    k_scale, k_normal, k = turned(k_raw, gain_k)
    return q_scale, q_normal, (q * HD ** (-0.5)).astype(BF), k_scale, k_normal, k.astype(BF)


def attention_forward_kernel(q_ref, k_ref, v_ref, gq, gk, cos, sin, row, col, out, q_s):
    _, _, q, _, _, k = attention_parts(q_ref[...], k_ref[...], gq[...], gk[...], cos[...], sin[...])
    v = v_ref[...].astype(BF)
    q_s[...] = q
    tile = 128

    def step(i, carry):
        rows = pl.ds(pl.multiple_of(i * tile, tile), tile)
        scores = mm_nt(q_s[rows, :], k)
        scores = jnp.where(col[rows, :] == row[...], scores, NEG)
        peak = jnp.max(scores, axis=-1, keepdims=True)
        expo = jnp.exp(scores - peak)
        probs = expo / jnp.sum(expo, axis=-1, keepdims=True)
        out[rows, :] = mm(probs.astype(BF), v).astype(BF)
        return carry

    lax.fori_loop(0, q_s.shape[0] // tile, step, 0)


def attention_forward(raw, gain_q, gain_k, cosine, sine, segments, heads):
    length = raw.shape[0]
    table = pl.BlockSpec((length, HD), lambda h: (0, 0))
    gain = pl.BlockSpec((1, HD), lambda h: (0, 0))

    def column(part):
        return pl.BlockSpec((length, HD), lambda h: (0, part * heads + h))

    return pl.pallas_call(
        attention_forward_kernel,
        grid=(heads,),
        in_specs=[column(0), column(1), column(2), gain, gain, table, table]
        + [
            pl.BlockSpec((1, length), lambda h: (0, 0)),
            pl.BlockSpec((length, 1), lambda h: (0, 0)),
        ],
        out_specs=pl.BlockSpec((length, HD), lambda h: (0, h)),
        out_shape=jax.ShapeDtypeStruct((length, heads * HD), BF),
        scratch_shapes=[pltpu.VMEM((length, HD), BF)],
        compiler_params=pltpu.CompilerParams(vmem_limit_bytes=24 << 20),
        cost_estimate=pl.CostEstimate(
            flops=4 * heads * length * length * HD,
            bytes_accessed=heads * length * HD * 14,
            transcendentals=heads * length * length,
        ),
        name="attention_forward",
    )(raw, raw, raw, gain_q, gain_k, cosine, sine, *segments)


def attention_backward_kernel(
    heads, q_ref, k_ref, v_ref, da_ref, gq, gk, cos, sin, row, col, out, gains, q_s, dq_s, dk_s, dv_s
):
    head = pl.program_id(0)
    q_scale, q_normal, q, k_scale, k_normal, k = attention_parts(
        q_ref[...], k_ref[...], gq[...], gk[...], cos[...], sin[...]
    )
    v = v_ref[...].astype(BF)
    q_s[...] = q
    dk_s[...] = jnp.zeros_like(dk_s)
    dv_s[...] = jnp.zeros_like(dv_s)
    tile = 128

    def step(i, carry):
        rows = pl.ds(pl.multiple_of(i * tile, tile), tile)
        qt = q_s[rows, :]
        da = da_ref[rows, :]
        scores = mm_nt(qt, k)
        scores = jnp.where(col[rows, :] == row[...], scores, NEG)
        peak = jnp.max(scores, axis=-1, keepdims=True)
        expo = jnp.exp(scores - peak)
        probs = expo / jnp.sum(expo, axis=-1, keepdims=True)
        prob_grad = mm_nt(da, v)
        inner = jnp.sum(probs * prob_grad, axis=-1, keepdims=True)
        score_grad = (probs * (prob_grad - inner)).astype(BF)
        dq_s[rows, :] = mm(score_grad, k)
        dk_s[...] += mm_tn(score_grad, qt)
        dv_s[...] += mm_tn(probs.astype(BF), da)
        return carry

    lax.fori_loop(0, q_s.shape[0] // tile, step, 0)
    cosine, sine = cos[...], sin[...]

    def back(grad, normal, scale, gain):
        turned = grad * cosine - pltpu.roll(grad, HD // 2, 1) * sine
        weighted = turned * gain
        inner = jnp.mean(weighted * normal, axis=-1, keepdims=True)
        return (scale * (weighted - normal * inner)).astype(BF), jnp.sum(
            turned * normal, axis=0, keepdims=True
        )

    dq, sum_q = back(dq_s[...] * HD ** (-0.5), q_normal, q_scale, gq[...])
    dk, sum_k = back(dk_s[...], k_normal, k_scale, gk[...])

    def place(part, value):
        out[:, pl.ds(pl.multiple_of((part * heads + head) * HD, HD), HD)] = value

    place(0, dq)
    place(1, dk)
    place(2, dv_s[...].astype(BF))

    @pl.when(head == 0)
    def _():
        gains[...] = jnp.zeros_like(gains)

    gains[0:1, :] += sum_q
    gains[1:2, :] += sum_k


def attention_backward(raw, grad, gain_q, gain_k, cosine, sine, segments, heads):
    length = raw.shape[0]
    table = pl.BlockSpec((length, HD), lambda h: (0, 0))
    gain = pl.BlockSpec((1, HD), lambda h: (0, 0))

    def column(part):
        return pl.BlockSpec((length, HD), lambda h: (0, part * heads + h))

    return pl.pallas_call(
        functools.partial(attention_backward_kernel, heads),
        grid=(heads,),
        in_specs=[column(0), column(1), column(2), column(0), gain, gain, table, table]
        + [
            pl.BlockSpec((1, length), lambda h: (0, 0)),
            pl.BlockSpec((length, 1), lambda h: (0, 0)),
        ],
        out_specs=[
            pl.BlockSpec((length, 3 * heads * HD), lambda h: (0, 0)),
            pl.BlockSpec((8, HD), lambda h: (0, 0)),
        ],
        out_shape=[
            jax.ShapeDtypeStruct((length, 3 * heads * HD), BF),
            jax.ShapeDtypeStruct((8, HD), F32),
        ],
        scratch_shapes=[pltpu.VMEM((length, HD), BF)] + [pltpu.VMEM((length, HD), F32)] * 3,
        compiler_params=pltpu.CompilerParams(vmem_limit_bytes=28 << 20),
        cost_estimate=pl.CostEstimate(
            flops=10 * heads * length * length * HD,
            bytes_accessed=heads * length * HD * 20,
            transcendentals=heads * length * length,
        ),
        name="attention_backward",
    )(raw, raw, raw, grad, gain_q, gain_k, cosine, sine, *segments)


def experts_kernel(places, n_tp, n_local, base, offsets, *refs):
    count = len(places)
    xp = refs[:count]
    g_hbm, pick, gate_up_hbm, down_hbm, own, oth, mid_out, grad_out = refs[count : count + 8]
    xs, gs, gate_up, down, gate_s, up_s, back_s, sems = refs[count + 8 :]
    rows = xs.shape[0]
    size = rows // count
    mids = down.shape[0]
    ffe = mids // n_local
    copies = []
    for i in range(count):
        at = pl.ds(i * size, size)
        copies.append(pltpu.make_async_copy(xp[i], xs.at[at], sems.at[i]))
        part = size // n_tp
        for m in range(n_tp):
            core, block, first = places[i]
            there = offsets[core, block] + first + (base[1] ^ m) * part
            copies.append(
                pltpu.make_async_copy(
                    g_hbm.at[pl.ds(pl.multiple_of(there, 8), part)],
                    gs.at[pl.ds(i * size + m * part, part)],
                    sems.at[count + i * n_tp + m],
                )
            )
    loads = []
    for e in range(n_local):
        for h in range(2):
            at = pl.ds(h * mids + e * ffe, ffe)
            loads.append(
                pltpu.make_async_copy(
                    gate_up_hbm.at[:, at], gate_up.at[:, at], sems.at[count * (n_tp + 1) + 3 * e + h]
                )
            )
        at = pl.ds(e * ffe, ffe)
        loads.append(
            pltpu.make_async_copy(down_hbm.at[at], down.at[at], sems.at[count * (n_tp + 1) + 3 * e + 2])
        )
    for c in copies + loads:
        c.start()
    for c in copies:
        c.wait()
    lane = lax.broadcasted_iota(jnp.int32, (1, SIDE), 1)
    half = rows // 2
    own[:, D:] = jnp.zeros((half, SIDE), BF)
    oth[:, D:] = jnp.zeros((half, SIDE), BF)
    tile = 64
    for e in range(n_local):
        for c in loads[3 * e : 3 * e + 3]:
            c.wait()
        at_gate = pl.ds(e * ffe, ffe)
        at_up = pl.ds(mids + e * ffe, ffe)
        gate_s[...] = mm(xs[:, :D], gate_up[:, at_gate])
        up_s[...] = mm(xs[:, :D], gate_up[:, at_up])
        back_s[...] = mm_nt(gs[...], down[at_gate, :])
        column = base[0] + e
        chosen = pick[e]
        for t in range(rows // tile):
            at = pl.ds(t * tile, tile)
            wide = mm(xs[at, D:], chosen)
            gate = gate_s[at, :]
            upper = up_s[at, :]
            back = back_s[at, :]
            sigma = 0.5 + 0.5 * jnp.tanh(0.5 * gate)
            active = gate * sigma
            mid = active * upper
            cot = jnp.sum(mid * back, axis=-1, keepdims=True)
            mid_out[at, at_gate] = (mid * wide).astype(BF)
            grad = back * wide
            grad_out[at, at_gate] = (grad * upper * (sigma + active * (1.0 - sigma))).astype(BF)
            grad_out[at, at_up] = (grad * active).astype(BF)
            high = cot.astype(BF).astype(F32)
            side = jnp.where(lane == column, high, 0.0)
            side = side + jnp.where(lane == column + LOW, cot - high, 0.0)
            to = own if t * tile < half else oth
            there = pl.ds(t * tile % half, tile)
            to[there, D:] = to[there, D:] + side.astype(BF)
    own[:, :D] = mm_nt(grad_out[pl.ds(0, half), :], gate_up[...]).astype(BF)
    oth[:, :D] = mm_nt(grad_out[pl.ds(half, half), :], gate_up[...]).astype(BF)


def experts(x_pieces, g_all, offsets, places, base, pick, gate_up, down):
    count = len(x_pieces)
    n_tp = lax.axis_size("tp")
    size, width = x_pieces[0].shape
    rows = count * size
    n_local = pick.shape[0]
    mids = down.shape[0]
    ffe = mids // n_local
    anywhere = pl.BlockSpec(memory_space=pl.ANY)

    def whole(*shape):
        return pl.BlockSpec(shape, lambda i, b, o: (0,) * len(shape))

    spec = pltpu.PrefetchScalarGridSpec(
        num_scalar_prefetch=2,
        grid=(1,),
        in_specs=[anywhere] * (count + 1) + [whole(*pick.shape), anywhere, anywhere],
        out_specs=[
            whole(rows // 2, width),
            whole(rows // 2, width),
            whole(rows, mids),
            whole(rows, 2 * mids),
        ],
        scratch_shapes=[
            pltpu.VMEM((rows, width), BF),
            pltpu.VMEM((rows, D), BF),
            pltpu.VMEM(gate_up.shape, BF),
            pltpu.VMEM(down.shape, BF),
            pltpu.VMEM((rows, ffe), F32),
            pltpu.VMEM((rows, ffe), F32),
            pltpu.VMEM((rows, ffe), F32),
            pltpu.SemaphoreType.DMA((count * (n_tp + 1) + 3 * n_local,)),
        ],
    )
    return pl.pallas_call(
        functools.partial(experts_kernel, tuple(places), n_tp, n_local),
        grid_spec=spec,
        out_shape=[
            jax.ShapeDtypeStruct((rows // 2, width), BF),
            jax.ShapeDtypeStruct((rows // 2, width), BF),
            jax.ShapeDtypeStruct((rows, mids), BF),
            jax.ShapeDtypeStruct((rows, 2 * mids), BF),
        ],
        compiler_params=pltpu.CompilerParams(vmem_limit_bytes=60 << 20),
        cost_estimate=pl.CostEstimate(
            flops=rows * mids * D * 10,
            bytes_accessed=6 * mids * D + rows * D * 10,
            transcendentals=rows * mids,
        ),
        name="experts",
    )(base, offsets, *x_pieces, g_all, pick, gate_up, down)

def weights_grad_kernel(places, n_tp, counts, offsets, own, *refs):
    n_x = len(places)
    xp = refs[:n_x]
    g_hbm = refs[n_x]
    n_c = len(counts)
    mids = refs[n_x + 1 : n_x + 1 + n_c]
    gates = refs[n_x + 1 + n_c : n_x + 1 + 2 * n_c]
    ups = refs[n_x + 1 + 2 * n_c : n_x + 1 + 3 * n_c]
    rest = refs[n_x + 1 + 3 * n_c :]
    gate_out, up_out, down_out, token, xs, gs, both, mid_s, sems = rest[-9:]
    token[...] = jnp.zeros_like(token)
    ffe = mid_s.shape[1]
    size = xs.shape[0] // n_x

    @pl.when(pl.program_id(0) == 0)
    def _():
        copies = []
        for i in range(n_x):
            at = pl.ds(i * size, size)
            copies.append(pltpu.make_async_copy(xp[i].at[:, pl.ds(0, D)], xs.at[at], sems.at[i]))
            part = size // n_tp
            for m in range(n_tp):
                core, block, first = places[i]
                there = offsets[core, block] + first + (own[0] ^ m) * part
                copies.append(
                    pltpu.make_async_copy(
                        g_hbm.at[pl.ds(pl.multiple_of(there, 8), part)],
                        gs.at[pl.ds(i * size + m * part, part)],
                        sems.at[n_x + i * n_tp + m],
                    )
                )
        for c in copies:
            c.start()
        for c in copies:
            c.wait()

    row = 0
    for c in range(n_c):
        at = pl.ds(row, counts[c])
        both[at, :ffe] = gates[c][...]
        both[at, ffe:] = ups[c][...]
        mid_s[at, :] = mids[c][...]
        row += counts[c]
    wide = 512

    def step(j, carry):
        at = pl.ds(pl.multiple_of(j * wide, wide), wide)
        part = mm_tn(xs[:, at], both[...])
        gate_out[0, at, :] = part[:, :ffe]
        up_out[0, at, :] = part[:, ffe:]
        down_out[0, :, at] = mm_tn(mid_s[...], gs[:, at])
        return carry

    lax.fori_loop(0, D // wide, step, 0)


def weights_grad(
    x_pieces, g_all, offsets, places, mids, grads, first, number, n_local, before
):
    size = x_pieces[0].shape[0]
    rows = size * len(x_pieces)
    ffe = mids[0].shape[1] // n_local
    counts = [m.shape[0] for m in mids]
    anywhere = pl.BlockSpec(memory_space=pl.ANY)

    def columns(count, shift):
        return pl.BlockSpec((count, ffe), lambda e, o, t: (0, shift + first + e))

    tall = pl.BlockSpec((1, D, ffe), lambda e, o, t: (first + e, 0, 0))
    flat = pl.BlockSpec((1, ffe, D), lambda e, o, t: (first + e, 0, 0))
    n_in = 3 + len(x_pieces) + 3 * len(mids)
    n_tp = lax.axis_size("tp")
    return pl.pallas_call(
        functools.partial(weights_grad_kernel, tuple(places), n_tp, tuple(counts)),
        grid_spec=pltpu.PrefetchScalarGridSpec(
            num_scalar_prefetch=2,
            grid=(number,),
            in_specs=[anywhere] * (len(x_pieces) + 1)
            + [columns(c, 0) for c in counts]
            + [columns(c, 0) for c in counts]
            + [columns(c, n_local) for c in counts]
            + [anywhere] * len(before),
            out_specs=[tall, tall, flat, pl.BlockSpec((8, 128), lambda e, o, t: (0, 0))],
            scratch_shapes=[
                pltpu.VMEM((rows, D), BF),
                pltpu.VMEM((rows, D), BF),
                pltpu.VMEM((rows, 2 * ffe), BF),
                pltpu.VMEM((rows, ffe), BF),
                pltpu.SemaphoreType.DMA((len(x_pieces) * (n_tp + 1),)),
            ],
        ),
        out_shape=[
            jax.ShapeDtypeStruct((n_local, D, ffe), F32),
            jax.ShapeDtypeStruct((n_local, D, ffe), F32),
            jax.ShapeDtypeStruct((n_local, ffe, D), F32),
            jax.ShapeDtypeStruct((8, 128), F32),
        ],
        input_output_aliases={n_in + i: i for i in range(len(before))},
        compiler_params=pltpu.CompilerParams(vmem_limit_bytes=62 << 20),
        cost_estimate=pl.CostEstimate(
            flops=6 * rows * D * ffe * number,
            bytes_accessed=4 * rows * D + 12 * D * ffe * number,
            transcendentals=0,
        ),
        name="weights_grad",
    )(offsets, tp_index(), *x_pieces, g_all, *mids, *grads, *grads, *before)


def prepare_kernel(core, q, k, v, o, gain, mine, theirs, out_mine, out_theirs):
    width = out_mine.shape[1]
    scale = gain[...].astype(F32)
    for to, out_to, which in ((mine, out_mine, core[0]), (theirs, out_theirs, 1 - core[0])):
        at = pl.ds(pl.multiple_of(which * width, width), width)
        for i, w in enumerate((q, k, v)):
            to[:, i * width : (i + 1) * width] = (w[:, at].astype(F32) * scale).astype(BF)
        out_to[...] = o[:, at]


def prepare(core, q, k, v, o, gain):
    depth, both = q.shape
    width = both // 2

    def whole(*shape):
        return pl.BlockSpec(shape, lambda i, c: (0,) * len(shape))

    return pl.pallas_call(
        prepare_kernel,
        grid_spec=pltpu.PrefetchScalarGridSpec(
            num_scalar_prefetch=1,
            grid=(1,),
            in_specs=[whole(depth, both)] * 4 + [whole(depth, 1)],
            out_specs=[whole(depth, 3 * width)] * 2 + [whole(depth, width)] * 2,
        ),
        out_shape=[jax.ShapeDtypeStruct((depth, 3 * width), BF)] * 2
        + [jax.ShapeDtypeStruct((depth, width), BF)] * 2,
        compiler_params=pltpu.CompilerParams(vmem_limit_bytes=16 << 20),
        name="prepare",
    )(core[None].astype(jnp.int32), q, k, v, o, gain)


def whole_spec(*shape):
    return pl.BlockSpec(shape, lambda *i: (0,) * len(shape))


ANYWHERE = pl.BlockSpec(memory_space=pl.ANY)


def first_norm_kernel(x, out):
    value = x[...].astype(F32)
    out[...] = (value * lax.rsqrt(jnp.mean(value * value, axis=-1, keepdims=True) + eps)).astype(BF)


def first_norm(x):
    rows = x.shape[0]
    tile = 96
    block = pl.BlockSpec((tile, D), lambda i: (i, 0))
    return pl.pallas_call(
        first_norm_kernel,
        grid=(rows // tile,),
        in_specs=[block],
        out_specs=block,
        out_shape=jax.ShapeDtypeStruct(x.shape, BF),
        compiler_params=pltpu.CompilerParams(vmem_limit_bytes=16 << 20),
        name="first_norm",
    )(x)


def fixed(*shape):
    return pl.BlockSpec(shape, lambda i, own: (0,) * len(shape))


def tp_index():
    return lax.axis_index("tp").astype(jnp.int32)[None]


def place_kernel(count, firsts, size, own, *refs):
    out = refs[-1]
    waves = len(firsts)
    for m in range(count):
        for w, first in enumerate(firsts):
            there = pl.multiple_of((w * count + (own[0] ^ m)) * size, 8)
            out[pl.ds(there, size), :] = refs[m * waves + w][first * size : (first + 1) * size, :]


def place(chunks, firsts, size, *deps):
    arrays = [a for c in chunks for a in c]
    width = arrays[0].shape[1]
    rows = size * len(arrays)
    return pl.pallas_call(
        functools.partial(place_kernel, len(chunks), tuple(firsts), size),
        grid_spec=pltpu.PrefetchScalarGridSpec(
            num_scalar_prefetch=1,
            grid=(1,),
            in_specs=[whole_spec(*a.shape) for a in arrays] + [ANYWHERE] * len(deps),
            out_specs=whole_spec(rows, width),
        ),
        out_shape=jax.ShapeDtypeStruct((rows, width), arrays[0].dtype),
        compiler_params=pltpu.CompilerParams(vmem_limit_bytes=24 << 20),
        name="place",
    )(tp_index(), *arrays, *deps)


def combine_kernel(counts, size, own, *refs):
    at = 0
    outs = refs[sum(sum(c) for c in counts) :]
    for segments, out in zip(counts, outs):
        for i, count in enumerate(segments):
            total = refs[at][...].astype(F32)
            for r in refs[at + 1 : at + count]:
                total = total + r[...].astype(F32)
            out[i * size : (i + 1) * size, :] = total.astype(out.dtype)
            at += count


def combine(outs, size, dtypes=None):
    dtypes = dtypes or [BF] * len(outs)
    terms = [t for segments in outs for s in segments for t in s]
    width = terms[0][0].shape[1]

    def rows(term):
        assert term[1] % size == 0
        at = term[1] // size
        if len(term) == 2:
            return pl.BlockSpec((size, width), lambda i, own: (at, 0))
        return pl.BlockSpec((size, width), lambda i, own: (at + (own[0] ^ term[2]), 0))

    return pl.pallas_call(
        functools.partial(combine_kernel, [[len(s) for s in o] for o in outs], size),
        grid_spec=pltpu.PrefetchScalarGridSpec(
            num_scalar_prefetch=1,
            grid=(1,),
            in_specs=[rows(t) for t in terms],
            out_specs=[fixed(size * len(o), width) for o in outs],
        ),
        out_shape=[
            jax.ShapeDtypeStruct((size * len(o), width), t) for o, t in zip(outs, dtypes)
        ],
        compiler_params=pltpu.CompilerParams(vmem_limit_bytes=20 << 20),
        name="combine",
    )(tp_index(), *[t[0] for t in terms])


def branch_kernel(count, *refs):
    down, out = refs[count:]
    row = 0
    for r in refs[:count]:
        size = r.shape[0]
        out[row : row + size, :] = mm(r[...], down[...]).astype(BF)
        row += size


def branch_rows(parts, half, down):
    sizes = [p.shape[0] // 2 for p in parts]
    mids = down.shape[0]

    def rows(size):
        return pl.BlockSpec((size, mids), lambda i: (half, 0))

    return pl.pallas_call(
        functools.partial(branch_kernel, len(parts)),
        grid=(1,),
        in_specs=[rows(s) for s in sizes] + [whole_spec(mids, D)],
        out_specs=whole_spec(sum(sizes), D),
        out_shape=jax.ShapeDtypeStruct((sum(sizes), D), BF),
        compiler_params=pltpu.CompilerParams(vmem_limit_bytes=28 << 20),
        cost_estimate=pl.CostEstimate(
            flops=2 * sum(sizes) * mids * D,
            bytes_accessed=2 * (sum(sizes) * (mids + D) + mids * D),
            transcendentals=0,
        ),
        name="branch_rows",
    )(*parts, down)


def inward_kernel(n_a, n_b, owners, *refs):
    pieces = refs[:n_a]
    blocks = refs[n_a : n_a + n_b]
    out = refs[-1]
    size = D // n_b
    row = 0
    for a in pieces:
        total = None
        for b in range(n_b):
            at = pl.ds(pl.multiple_of(owners[b] * size, size), size)
            part = mm(a[:, at], blocks[b][:size, :])
            total = part if total is None else total + part
        out[row : row + a.shape[0], :] = total.astype(out.dtype)
        row += a.shape[0]


def inward(pieces, blocks, owners, dtype):
    rows = sum(a.shape[0] for a in pieces)
    width = blocks[0].shape[1]
    return pl.pallas_call(
        functools.partial(inward_kernel, len(pieces), len(blocks)),
        grid_spec=pltpu.PrefetchScalarGridSpec(
            num_scalar_prefetch=1,
            grid=(1,),
            in_specs=[whole_spec(*a.shape) for a in pieces]
            + [whole_spec(*b.shape) for b in blocks],
            out_specs=whole_spec(rows, width),
        ),
        out_shape=jax.ShapeDtypeStruct((rows, width), dtype),
        compiler_params=pltpu.CompilerParams(vmem_limit_bytes=24 << 20),
        cost_estimate=pl.CostEstimate(
            flops=2 * rows * D * width,
            bytes_accessed=2 * (rows * D + D * width) + 4 * rows * width,
            transcendentals=0,
        ),
        name="inward",
    )(owners, *pieces, *blocks)


def outward_kernel(n_b, owners, a, *refs):
    blocks = refs[:n_b]
    out = refs[-1]
    size = D // n_b
    for b in range(n_b):
        at = pl.ds(pl.multiple_of(owners[b] * size, size), size)
        out[:, at] = mm_nt(a[...], blocks[b][:size, :]).astype(out.dtype)


def outward(a, half, blocks, owners, dtype):
    rows, width = a.shape[0] // 2, a.shape[1]
    return pl.pallas_call(
        functools.partial(outward_kernel, len(blocks)),
        grid_spec=pltpu.PrefetchScalarGridSpec(
            num_scalar_prefetch=1,
            grid=(1,),
            in_specs=[pl.BlockSpec((rows, width), lambda i, o: (half, 0))]
            + [whole_spec(*b.shape) for b in blocks],
            out_specs=whole_spec(rows, D),
        ),
        out_shape=jax.ShapeDtypeStruct((rows, D), dtype),
        compiler_params=pltpu.CompilerParams(vmem_limit_bytes=24 << 20),
        cost_estimate=pl.CostEstimate(
            flops=2 * rows * D * width,
            bytes_accessed=2 * (rows * width + D * width) + 4 * rows * D,
            transcendentals=0,
        ),
        name="outward",
    )(owners, a, *blocks)


def matrix_grad_kernel(n_a, n_b, *refs):
    pieces = refs[:n_a]
    grad, out = refs[n_a], refs[-1]
    size = D // n_b
    for b in range(n_b):
        at = slice(b * size, (b + 1) * size)
        total = None
        row = 0
        for a in pieces:
            part = mm_tn(a[:, at], grad[row : row + a.shape[0], :])
            total = part if total is None else total + part
            row += a.shape[0]
        out[at, :] = total.astype(BF)


def matrix_grad(pieces, grad, *deps):
    rows, width = grad.shape
    return pl.pallas_call(
        functools.partial(matrix_grad_kernel, len(pieces), 4),
        grid=(1,),
        in_specs=[whole_spec(*a.shape) for a in pieces]
        + [whole_spec(rows, width)]
        + [ANYWHERE] * len(deps),
        out_specs=whole_spec(D, width),
        out_shape=jax.ShapeDtypeStruct((D, width), BF),
        compiler_params=pltpu.CompilerParams(vmem_limit_bytes=24 << 20),
        cost_estimate=pl.CostEstimate(
            flops=2 * rows * D * width,
            bytes_accessed=2 * (rows * D + D * width + rows * width),
            transcendentals=0,
        ),
        name="matrix_grad",
    )(*pieces, grad, *deps)


def second_norm_kernel(n_got, index, *refs):
    own = refs[0]
    got = refs[1 : 1 + n_got]
    x, gain, router, routes, residual_out, payload_out, gates_out = refs[1 + n_got :]
    residual = own[...]
    for r in got:
        residual = residual + r[...].astype(F32)
    residual = residual + x[...].astype(F32)
    scale = lax.rsqrt(jnp.mean(residual * residual, axis=-1, keepdims=True) + eps)
    hidden = (residual * scale * gain[...]).astype(BF)
    logits = mm_nt(hidden, router[...])
    rows = hidden.shape[0]
    lane = lax.broadcasted_iota(jnp.int32, (rows, SIDE), 1)
    named = lane == routes[:, 0:1]
    for k in range(1, TOP):
        named = named | (lane == routes[:, k : k + 1])
    logits = jnp.where(named, logits, NEG)
    top = jnp.max(logits, axis=-1, keepdims=True)
    expo = jnp.where(named, jnp.exp(logits - top), 0.0)
    gates = expo / jnp.sum(expo, axis=-1, keepdims=True)
    high = gates.astype(BF)
    low = gates - high.astype(F32)
    residual_out[...] = residual
    gates_out[...] = gates
    payload_out[:, :D] = hidden
    payload_out[:, D:] = (high.astype(F32) + pltpu.roll(low, LOW, 1)).astype(BF)


def second_norm(own, got, x, gain, router, routes):
    rows = own.shape[0]
    count = len(got) + 1
    return pl.pallas_call(
        functools.partial(second_norm_kernel, len(got)),
        grid_spec=pltpu.PrefetchScalarGridSpec(
            num_scalar_prefetch=1,
            grid=(1,),
            in_specs=[fixed(rows, D)] * count
            + [fixed(rows, D), fixed(1, D), fixed(SIDE, D), fixed(rows, TOP)],
            out_specs=[fixed(rows, D), fixed(rows, D + SIDE), fixed(rows, SIDE)],
        ),
        out_shape=[
            jax.ShapeDtypeStruct((rows, D), F32),
            jax.ShapeDtypeStruct((rows, D + SIDE), BF),
            jax.ShapeDtypeStruct((rows, SIDE), F32),
        ],
        compiler_params=pltpu.CompilerParams(vmem_limit_bytes=16 << 20),
        name="second_norm",
    )(tp_index(), own, *got, x, gain, router, routes)


def second_norm_back_kernel(n_got, index, *refs):
    own = refs[0]
    got = refs[1 : 1 + n_got]
    residual_in, payload, gates_in, cot, gain, router, grad_out, low_out, small_out = refs[1 + n_got :]
    total = own[...]
    for r in got:
        total = total + r[...].astype(F32)
    side = total[:, D:]
    lane = lax.broadcasted_iota(jnp.int32, side.shape, 1)
    gates = gates_in[...]
    gate_cot = jnp.where(lane < LOW, side + pltpu.roll(side, LOW, 1), 0.0)
    inner = jnp.sum(gates * gate_cot, axis=-1, keepdims=True)
    logit_grad = (gates * (gate_cot - inner)).astype(BF)
    hidden_grad = total[:, :D] + mm(logit_grad, router[...])
    residual = residual_in[...]
    scale = lax.rsqrt(jnp.mean(residual * residual, axis=-1, keepdims=True) + eps)
    normal = residual * scale
    weighted = hidden_grad * gain[...]
    inner = jnp.mean(weighted * normal, axis=-1, keepdims=True)
    grad = cot[...].astype(F32) + scale * (weighted - normal * inner)
    grad_out[...] = grad
    low_out[...] = grad.astype(BF)
    small_out[0:SIDE, :] = mm_tn(logit_grad, payload[:, :D])
    small_out[SIDE : SIDE + 8, :] = jnp.broadcast_to(
        jnp.sum(hidden_grad * normal, axis=0, keepdims=True), (8, D)
    )


def second_norm_back(own, got, residual, payload, gates, cot, gain, router):
    rows = own.shape[0]
    count = len(got) + 1
    return pl.pallas_call(
        functools.partial(second_norm_back_kernel, len(got)),
        grid_spec=pltpu.PrefetchScalarGridSpec(
            num_scalar_prefetch=1,
            grid=(1,),
            in_specs=[fixed(rows, D + SIDE)] * count
            + [fixed(rows, D), fixed(rows, D + SIDE), fixed(rows, SIDE)]
            + [fixed(rows, D), fixed(1, D), fixed(SIDE, D)],
            out_specs=[fixed(rows, D), fixed(rows, D), fixed(SIDE + 8, D)],
        ),
        out_shape=[
            jax.ShapeDtypeStruct((rows, D), F32),
            jax.ShapeDtypeStruct((rows, D), BF),
            jax.ShapeDtypeStruct((SIDE + 8, D), F32),
        ],
        compiler_params=pltpu.CompilerParams(vmem_limit_bytes=20 << 20),
        name="second_norm_back",
    )(tp_index(), own, *got, residual, payload, gates, cot, gain, router)


def input_grad_kernel(n_got, n_waves, index, *refs):
    own = refs[0]
    got = refs[1 : 1 + n_got]
    x_in = refs[1 + n_got : 1 + n_got + n_waves]
    grads = refs[1 + n_got + n_waves : 1 + n_got + 2 * n_waves]
    residual, out = refs[1 + n_got + 2 * n_waves], refs[-1]
    total = own[...]
    for r in got:
        total = total + r[...].astype(F32)
    row = 0
    for x_ref, g in zip(x_in, grads):
        size = g.shape[0]
        weighted = total[row : row + size]
        x = x_ref[...].astype(F32)
        scale = lax.rsqrt(jnp.mean(x * x, axis=-1, keepdims=True) + eps)
        normal = x * scale
        inner = jnp.mean(weighted * normal, axis=-1, keepdims=True)
        out[row : row + size, :] = (g[...] + scale * (weighted - normal * inner)).astype(BF)
        row += size
    out[row:, :] = (residual[...] + total[row:]).astype(BF)


def input_grad_rows(own, got, x, grads, residual, *deps):
    size = residual.shape[0]
    count = len(got) + 1
    waves = len(grads)
    return pl.pallas_call(
        functools.partial(input_grad_kernel, len(got), waves),
        grid_spec=pltpu.PrefetchScalarGridSpec(
            num_scalar_prefetch=1,
            grid=(1,),
            in_specs=[fixed(*own.shape)] * count
            + [fixed(size, D)] * (2 * waves + 1)
            + [ANYWHERE] * len(deps),
            out_specs=fixed(*own.shape),
        ),
        out_shape=jax.ShapeDtypeStruct(own.shape, BF),
        compiler_params=pltpu.CompilerParams(vmem_limit_bytes=20 << 20),
        name="input_grad_rows",
    )(tp_index(), own, *got, *x, *grads, residual, *deps)


def local(
    tokens,
    segment_ids,
    routes,
    norm1_gain,
    q_weight,
    k_weight,
    v_weight,
    q_gain,
    k_gain,
    out_weight,
    norm2_gain,
    router_weight,
    gate_weights,
    up_weights,
    down_weights,
    out_cotangent,
):
    rows = tokens.shape[0]
    n_experts = router_weight.shape[1]
    n_local, _, ffe = gate_weights.shape
    width = q_weight.shape[1] // 2
    heads = width // HD
    depth = q_weight.shape[0]
    per = q_gain.shape[0]
    core = lax.axis_index("ctx")
    place_f = lax.axis_index("fsdp")
    group = place_f * 2 + core
    n_f = lax.axis_size("fsdp")
    n_tp = lax.axis_size("tp")
    wave = rows // WAVES
    chunk = wave // n_tp
    mids = n_local * ffe
    if n_f == 4:
        owners = place_f ^ jnp.stack([0 * core, 1 + core, 2 - core, 0 * core + 3])
    else:
        owners = jnp.arange(n_f)
    owners = owners.astype(jnp.int32)

    if n_f == 4:
        other_owners = place_f ^ jnp.stack([0 * core, 2 - core, 1 + core, 0 * core + 3])
    else:
        other_owners = owners
    cot_rows = rows * jnp.stack([owners * 2 + core, other_owners * 2 + (1 - core)])
    cot_rows = cot_rows.astype(jnp.int32)

    gain_one = f32(norm1_gain)[:, None]
    qkv_mine, qkv_theirs, out_mine, out_theirs = prepare(
        core, q_weight, k_weight, v_weight, out_weight, norm1_gain[:, None]
    )
    small_rows = -(-(n_experts + 16) // 16) * 16
    small = jnp.concatenate(
        [
            jnp.pad(q_gain, (0, depth - per))[None, :],
            jnp.pad(k_gain, (0, depth - per))[None, :],
            norm2_gain[None, :],
            jnp.zeros((13, depth), BF),
            router_weight.T,
            jnp.zeros((small_rows - n_experts - 16, depth), BF),
        ],
        axis=0,
    )
    qkv_block = in_order(qkv_mine, swap_ctx(qkv_theirs), 0)
    tokens, out_cotangent, segment_ids, routes = after(
        (tokens, out_cotangent, segment_ids, routes), qkv_block
    )
    normed_own = first_norm(tokens)
    normed = [normed_own, swap_ctx(normed_own)]
    small_all = lax.all_gather(after(small, normed_own), ("fsdp", "ctx"), axis=0)
    positions = lax.rem(core * rows + jnp.arange(2 * rows, dtype=jnp.int32), 2 * rows)
    cosine, sine = rotary_tables(after(positions, qkv_block), HD)
    segments = lax.dynamic_slice_in_dim(
        jnp.concatenate([segment_ids[0], segment_ids[0]]), core * rows, 2 * rows
    )
    segments = (segments[None, :], segments[:, None])
    base = jnp.stack([group * n_local, lax.axis_index("tp")]).astype(jnp.int32)
    columns = base[0] + jnp.arange(n_local, dtype=jnp.int32)[:, None, None]
    lanes = jnp.arange(SIDE, dtype=jnp.int32)[None, :, None]
    pick = bf(
        jnp.broadcast_to((lanes == columns) | (lanes == columns + LOW), (n_local, SIDE, ffe))
    )
    def rows_of_waves(a):
        own = lax.axis_index("tp") * chunk
        return [lax.dynamic_slice_in_dim(a, w * wave + own, chunk) for w in range(WAVES)]

    x_rows, cot_own, routes_own = [rows_of_waves(a) for a in (tokens, out_cotangent, routes)]
    out_block = in_order(out_mine, swap_ctx(out_theirs), 0)
    qkv_blocks = gather_f(
        qkv_block, (normed_own, cosine, sine, segments, x_rows, cot_own, routes_own, small_all)
    )
    out_blocks = gather_f(after(out_block, qkv_blocks[-1]), (pick, cot_rows))
    cot_all = lax.all_gather(
        after(out_cotangent, qkv_blocks[-1]),
        ("fsdp", "ctx"),
        axis=0,
        tiled=True,
    )
    gain_q = f32(small_all[:, 0, :per].reshape(1, HD))
    gain_k = f32(small_all[:, 1, :per].reshape(1, HD))
    gain_two = f32(small_all[:, 2].reshape(1, D))
    router_wide = jnp.concatenate(
        [
            jnp.swapaxes(small_all[:, 16 : 16 + n_experts], 0, 1).reshape(n_experts, D),
            jnp.zeros((SIDE - n_experts, D), BF),
        ],
        axis=0,
    )
    raw = inward(normed, qkv_blocks, owners, F32)
    attended = attention_forward(raw, gain_q, gain_k, cosine, sine, segments, heads)
    attn_give = outward(attended, 1, out_blocks, owners, BF)
    attn_got = swap_ctx(attn_give)
    attn_keep = outward(after(attended, attn_give), 0, out_blocks, owners, F32)

    def tp_hops(sends):
        return [hop_tp(a, m + 1) for m, a in enumerate(sends)]

    down = down_weights.reshape(mids, D)
    residuals, payloads, gates_own, hid_pieces = [], [], [], []

    def attention_sums(w, *order):
        keep, got = after((attn_keep, attn_got), *order)
        lo = w * wave
        own, *sends = combine(
            [[[(keep, lo, m), (got, lo, m)]] for m in range(n_tp)],
            chunk,
            [F32] + [BF] * (n_tp - 1),
        )
        return own, sends, tp_hops(sends)

    def norm_rows(w, own, got):
        residual, payload, gates = second_norm(
            own, got, x_rows[w], gain_two, router_wide, routes_own[w]
        )
        residuals.append(residual)
        payloads.append(payload)
        gates_own.append(gates)
        return gather_tp(payload)

    def both_cores(a, *order):
        return a, swap_ctx(after(a, *order) if order else a)

    def gather_wave(chunks):
        payload = jnp.concatenate(chunks, axis=0)
        if n_f != 4:
            hid_pieces.append([both_cores(b) for b in gather_f(payload)])
            return payload, None
        near = gather_near(payload)
        hid_pieces.append([both_cores(payload, near[1])])
        return payload, near

    own_rows, sends, got_rows = attention_sums(0)
    gate_in, up_in = after((gate_weights, up_weights), *sends)
    gate_up = jnp.concatenate(
        [
            jnp.transpose(gate_in, (1, 0, 2)).reshape(D, mids),
            jnp.transpose(up_in, (1, 0, 2)).reshape(D, mids),
        ],
        axis=1,
    )
    own_rows = after(own_rows, gate_up, pick)
    payload, near_a = gather_wave(norm_rows(0, own_rows, got_rows))
    own_rows, _, got_rows = attention_sums(1, payload)
    assert WAVES == 2

    kept = []

    def call(w, blocks, *order):
        xs = [hid_pieces[w][b][s] for s in range(2) for b in blocks]
        at = [(s, b, w * wave) for s in range(2) for b in blocks]
        if order:
            xs[0] = after(xs[0], *order)
        own, oth, mid, grads = experts(
            xs, cot_all, cot_rows, at, base, pick, gate_up, down
        )
        kept.append((xs, at, mid, grads, blocks, w))
        return own, oth

    def swapped(blocks, own, oth, *order):
        if order:
            oth = after(oth, *order)
        got = swap_ctx(oth)
        return {b: [(own, i * wave), (got, i * wave)] for i, b in enumerate(blocks)}

    def branch_half(w, s, *order):
        parts = [k[2] for k in kept if k[5] == w]
        places = [b for k in kept if k[5] == w for b in k[4]]
        parts[0] = after(parts[0], *order)
        return branch_rows(parts, s, down), places

    def branch_terms(keep, got, places):
        return {b: [(keep, i * wave), (got, i * wave)] for i, b in enumerate(places)}

    def tied(terms, *order):
        return [(after(terms[0][0], *order), terms[0][1])] + list(terms[1:])

    def shifted(terms, row):
        return [(a, at + row) for a, at in terms]

    def tp_parts(terms, *order):
        terms = tied(terms, *order)
        parts = combine(
            [[shifted(terms, m * chunk)] for m in range(n_tp)], chunk, [F32] + [BF] * (n_tp - 1)
        )
        return parts[0], parts[1:]

    def plain_terms(terms):
        return [a[at : at + wave] for a, at in terms]

    residual_grads, branch_pieces, small_parts = [], [], []

    def norm_back(w, parts, *order):
        own, sends = parts
        residual_grad, low, small_part = second_norm_back(
            after(own, *order) if order else own,
            tp_hops(sends),
            residuals[w],
            payloads[w],
            gates_own[w],
            cot_own[w],
            gain_two,
            router_wide,
        )
        residual_grads.append(residual_grad)
        small_parts.append(small_part)
        return low

    if n_f == 4:
        hid_pieces[0] += [both_cores(a) for a in near_a[1:]]
        far = gather_far(near_a)
        own_a, oth_a = call(0, [0, 1, 2])
        chunks = norm_rows(1, after(own_rows, own_a), got_rows)
        hid_pieces[0].append(both_cores(far, chunks[0]))
        own_f, oth_f = call(0, [3], own_a, chunks[0])
        payload, near_b = gather_wave([after(chunks[0], own_f)] + chunks[1:])
        terms_a = swapped([3], own_f, oth_f, payload)
        terms_a.update(swapped([0, 1, 2], own_a, oth_a, payload))
        give_a, places = branch_half(0, 1, payload)
        branch_got_a = swap_ctx(give_a)
        (far_a,) = combine([[tied(terms_a[3], give_a)]], wave)
        relay_a = hop_f(far_a, SIDEWAYS)
        keep_a, _ = branch_half(0, 0, far_a)
        branch_a = branch_terms(keep_a, branch_got_a, places)

        far = gather_far(near_b, keep_a)
        own_0, oth_0 = call(1, [0], keep_a)
        hid_pieces[1] += [both_cores(a, own_0) for a in near_b[1:]]
        hid_pieces[1].append(both_cores(far, own_0))
        send_1, send_2 = combine(
            [[tied(terms_a[1], own_0) + [(relay_a, 0)]], [terms_a[2]]], wave
        )
        terms_b = swapped([0], own_0, oth_0, send_1)
        feature = terms_a[0] + [(hop_f(send_1, NEAR), 0), (hop_f(send_2, SIDEWAYS), 0)]
        (branch_far,) = combine([[tied(branch_a[3], send_1)]], wave)
        branch_relay = hop_f(branch_far, SIDEWAYS)

        own_1, oth_1 = call(1, [1, 2], send_1, branch_far)
        feature_a = tp_parts(feature, own_1)
        terms_b.update(swapped([1, 2], own_1, oth_1, feature_a[0]))
        send_1, send_2 = combine(
            [[tied(branch_a[1], feature_a[0]) + [(branch_relay, 0)]], [branch_a[2]]], wave
        )
        branch = branch_a[0] + [(hop_f(send_1, NEAR), 0), (hop_f(send_2, SIDEWAYS), 0)]

        own_3, oth_3 = call(1, [3], own_1, send_1)
        low = norm_back(0, feature_a, own_3, branch[-1][0], branch[-2][0])
        terms_b.update(swapped([3], own_3, oth_3, low))
        own_g, *sends = combine(
            [[[(low, 0)], shifted(branch, m * chunk)] for m in range(n_tp)],
            chunk,
            [F32] + [BF] * (n_tp - 1),
        )
        got_g = tp_hops(sends)
        (far_b,) = combine([[tied(terms_b[3], own_g)]], wave)
        relay_b = hop_f(far_b, SIDEWAYS)
        send_1, send_2 = combine(
            [[tied(terms_b[1], far_b, got_g[0]) + [(relay_b, 0)]], [terms_b[2]]], wave
        )
        feature = terms_b[0] + [(hop_f(send_1, NEAR), 0), (hop_f(send_2, SIDEWAYS), 0)]
        (out_0,) = combine(
            [[[(residuals[0], 0), (after(own_g, send_1), chunk)] + [(a, chunk) for a in got_g]]],
            chunk,
        )
        branch_own = place([[low]] + [[a] for a in after(tuple(got_g), out_0)], (0,), chunk)
        branch_pieces.append((branch_own, swap_ctx(branch_own)))
        feature_b = tp_parts(tied(feature, out_0))
        give_b, places = branch_half(1, 1, feature_b[0])
        branch_got_b = swap_ctx(give_b)
        keep_b, _ = branch_half(1, 0, give_b)
        branch_b = branch_terms(keep_b, branch_got_b, places)
        (branch_far,) = combine([[branch_b[3]]], wave)
        branch_relay = hop_f(branch_far, SIDEWAYS)
        low = norm_back(1, feature_b)
        send_1, send_2 = combine(
            [[tied(branch_b[1], low) + [(branch_relay, 0)]], [branch_b[2]]], wave
        )
        last_branch = branch_b[0] + [(hop_f(send_1, NEAR), 0), (hop_f(send_2, SIDEWAYS), 0)]
        branch_own = place([[a] for a in gather_tp(low)], (0,), chunk)
        branch_pieces.append((branch_own, swap_ctx(branch_own)))
        out_chunks = gather_tp(after(out_0, branch_own))
        early = (send_1,)
        under = tuple(out_chunks[1:]) + tuple(a for a, _ in last_branch[-2:])
    else:
        for w in range(WAVES):
            if w == 1:
                gather_wave(norm_rows(1, own_rows, got_rows))
            terms = {}
            for b in range(n_f):
                terms.update(swapped([b], *call(w, [b])))
            got = reduce_f([plain_terms(terms[b]) for b in range(n_f)])
            low = norm_back(w, tp_parts([(a, 0) for a in got]))
            branch_own = place([[a] for a in gather_tp(low)], (0,), chunk)
            branch_pieces.append((branch_own, swap_ctx(branch_own)))
            give, places = branch_half(w, 1)
            keep, _ = branch_half(w, 0)
            terms = branch_terms(keep, swap_ctx(give), places)
            got = reduce_f([plain_terms(terms[b]) for b in range(n_f)])
            last_branch = [(a, 0) for a in got]
            if w == 0:
                own, sends = tp_parts(last_branch)
                (out_0,) = combine(
                    [[[(a, 0) for a in (residuals[0], own, *tp_hops(sends))]]], chunk
                )
                out_chunks = gather_tp(out_0)
        early = ()
        under = ()
    branch_grad = [branch_pieces[w][s] for s in range(2) for w in range(WAVES)]
    branch_grad[0] = after(branch_grad[0], *early)

    attended_grad = inward(branch_grad, out_blocks, owners, BF)
    out_grad_part = matrix_grad(branch_grad, attended, attended_grad)
    out_sum = lax.psum_scatter(out_grad_part, "fsdp", scatter_dimension=0, tiled=True)
    raw_grad, gain_terms = attention_backward(
        raw,
        after(attended_grad, out_grad_part),
        gain_q,
        gain_k,
        cosine,
        sine,
        segments,
        heads,
    )
    raw_grad = after(raw_grad, *under)
    normed_give = outward(raw_grad, 1, qkv_blocks, owners, BF)
    normed_got = swap_ctx(normed_give)
    qkv_grad_part = matrix_grad(normed, raw_grad, normed_give)
    qkv_sum = lax.psum_scatter(qkv_grad_part, "fsdp", scatter_dimension=0, tiled=True)
    normed_keep = outward(after(raw_grad, qkv_grad_part), 0, qkv_blocks, owners, F32)

    normed_rows, *normed_sends = combine(
        [
            [
                [(normed_keep, w * wave, m), (normed_got, w * wave, m)]
                for w in range(WAVES)
            ]
            + [shifted(last_branch, m * chunk)]
            for m in range(n_tp)
        ],
        chunk,
        [F32] + [BF] * (n_tp - 1),
    )
    normed_recv = tp_hops(normed_sends)

    small_parts, gain_terms = after((small_parts, gain_terms), *normed_sends)
    def spread(terms):
        return jnp.pad(terms.reshape(2 * n_f, per), ((0, 0), (0, depth - per))).reshape(1, D)

    small_grad = sum(small_parts)
    small_part = jnp.concatenate(
        [
            small_grad[:n_experts],
            small_grad[SIDE : SIDE + 1],
            spread(gain_terms[0]),
            spread(gain_terms[1]),
            jnp.zeros((small_rows - n_experts - 3, D), F32),
        ],
        axis=0,
    )
    small_part = jnp.swapaxes(small_part.reshape(small_rows, 2 * n_f, depth), 0, 1)
    small_sum = lax.psum_scatter(
        small_part.reshape(2 * n_f * small_rows, depth),
        ("fsdp", "ctx"),
        scatter_dimension=0,
        tiled=True,
    )

    def own_weight(mine):
        mine = f32(mine)
        keep = lax.dynamic_slice_in_dim(mine, core * depth, depth)
        give = lax.dynamic_slice_in_dim(mine, (1 - core) * depth, depth)
        return keep, f32(swap_ctx(bf(give)))

    x_pieces = [x for k in kept for x in k[0]]
    places = [p for k in kept for p in k[1]]
    mid_list = [k[2] for k in kept]
    grad_list = [k[3] for k in kept]
    def finish(rows_in, *order):
        rows_out = input_grad_rows(
            normed_rows, rows_in, x_rows, residual_grads, residuals[-1], *order
        )
        return rows_out, gather_tp(rows_out)

    if n_f == 4:
        step = n_local // 2
        x_pieces[0] = after(x_pieces[0], *normed_sends)
        *done, token = weights_grad(
            x_pieces, cot_all, cot_rows, places, mid_list, grad_list, 0, step, n_local, []
        )
        last_rows, last_chunks = finish(normed_recv, token, out_sum, qkv_sum)
        x_pieces[0] = after(x_pieces[0], last_rows)
        qkv_sum, out_sum = after((qkv_sum, out_sum), last_rows)
        *done, token = weights_grad(
            x_pieces, cot_all, cot_rows, places, mid_list, grad_list, step, n_local - step, n_local, done
        )
        ending = (token,)
    else:
        last_rows, last_chunks = finish(normed_recv)
        ending = ()
        x_all = jnp.concatenate([x[:, :D] for x in x_pieces], axis=0)
        own = lax.axis_index("tp")
        g_all = jnp.concatenate(
            [
                lax.dynamic_slice_in_dim(
                    cot_all, cot_rows[s, b] + first + (own ^ m) * chunk, chunk
                )
                for s, b, first in places
                for m in range(n_tp)
            ],
            axis=0,
        )
        grad_all = jnp.concatenate(grad_list, axis=0)
        mid_all = jnp.concatenate(mid_list, axis=0)
        done = [
            jnp.stack(
                [
                    mm_tn(x_all, grad_all[:, s * mids + e * ffe : s * mids + (e + 1) * ffe])
                    for e in range(n_local)
                ]
            )
            for s in range(2)
        ] + [mm_tn(mid_all, g_all).reshape(n_local, ffe, D)]
    input_grad = place([[c] * WAVES for c in last_chunks], range(WAVES), chunk, *ending)
    output = place([[o, c] for o, c in zip(out_chunks, last_chunks)], (0, WAVES), chunk)
    gate_grads, up_grads, down_grads = done

    qkv_keep, qkv_got = own_weight(qkv_sum)
    out_grad = in_order(*own_weight(out_sum), 1)
    plain = [
        in_order(
            qkv_keep[:, i * width : (i + 1) * width], qkv_got[:, i * width : (i + 1) * width], 1
        )
        for i in range(3)
    ]
    qkv_grads = [p * gain_one for p in plain]
    gain_one_part = sum(
        jnp.sum(p * f32(w), axis=1) for p, w in zip(plain, (q_weight, k_weight, v_weight))
    )

    small_sum = jnp.concatenate([small_sum, gain_one_part[None, :]], axis=0)
    small_sum = sum_of(gather_tp(after(small_sum, *last_chunks[1:])))
    return (
        output,
        input_grad,
        small_sum[small_rows],
        qkv_grads[0],
        qkv_grads[1],
        qkv_grads[2],
        small_sum[n_experts + 1, :per],
        small_sum[n_experts + 2, :per],
        out_grad,
        small_sum[n_experts],
        small_sum[:n_experts].T,
        gate_grads,
        up_grads,
        down_grads,
    )


def solution(mesh):
    both = ("fsdp", "ctx")
    in_specs = (
        P(both, None),
        P("fsdp", None),
        P(both, None),
        P(both),
        P(both, "tp"),
        P(both, "tp"),
        P(both, "tp"),
        P(both),
        P(both),
        P(both, "tp"),
        P(both),
        P(both, None),
        P(both, None, "tp"),
        P(both, None, "tp"),
        P(both, "tp", None),
        P(both, None),
    )
    out_specs = (
        P(both, None),
        P(both, None),
        P(both),
        P(both, "tp"),
        P(both, "tp"),
        P(both, "tp"),
        P(both),
        P(both),
        P(both, "tp"),
        P(both),
        P(both, None),
        P(both, None, "tp"),
        P(both, None, "tp"),
        P(both, "tp", None),
    )
    return jax.shard_map(local, mesh=mesh, in_specs=in_specs, out_specs=out_specs, check_vma=False)
```
